256 devices in a mesh: st: 16 (over y, x), tp: 16 (over z, core).
Axes of the slice: x: 4, y: 4, z: 8, core: 2. Of those that a mesh axis runs over, the one named last changes fastest.
Arguments:
- continuous: bfloat16 [512, 3, 1424], P(('st', 'tp')), may hold values from -48 to 48
- templates: bfloat16 [512, 12, 3, 400], P(('st', 'tp')), may hold values from -120 to 120
- station_list: int32 [512, 12], P(('st', 'tp')), may hold values from 0 to 511, as said below
- moveouts: int32 [512, 12], P(('st', 'tp')), may hold values from 0 to 256
Outputs:
- detection: float32 [512, 768], P(('st', 'tp'))
The draws below stay inside these ranges and needn't reach their ends.
Inputs may be any that keep to these rules, and one draw needn't show every extreme that they name: `station_list`: A station's group is station // 32. The 12 stations of a template are distinct, and so are their indices within their groups (station % 32). The rows of one device (2 templates, aligned blocks in order) name at most 3 stations of any one group, and in every such block one group is named exactly 3 times; blocks b and b2 with b % 16 == b2 % 16 share that group.
All inputs are finite; a program needn't handle non-finite values.
Results may differ from the reference program's by a relative error of at most 0.0003.
Values may be sent and summed in bfloat16 or wider, within the bound.
No kernel may reach another device: no remote copies, remote signals or barrier semaphores. Data moves between devices by JAX's collectives and lax.ppermute only.
A program may use at most 64 MiB of HBM per device.

```python
import math
import jax
import jax.numpy as jnp
from jax import lax

TPL_DEV = 2
WIN = 768
TLEN = 400
SHIFT_MAX = 256
CH = 3
NLIST = 12
GROUPS = 16
TGROUPS = 16
STA_GRP = 32
STATIONS = 512
TEMPLATES = 512
CAP = 3
OUT = 1024
DLEN = 1424


def rough_envelope(key, leading, length, block_size, lower, upper):
    block_total = (length + block_size - 1) // block_size
    levels = jnp.exp(jax.random.uniform(key, leading + (block_total,), jnp.float32, math.log(lower), math.log(upper)))
    return jnp.repeat(levels, block_size, axis=-1, total_repeat_length=block_total * block_size)[..., :length]


def draw_continuous(key, part):
    key_wave, key_scale, key_env = jax.random.split(key, 3)
    shape = (STATIONS, CH, DLEN)
    wave = jnp.clip(jax.random.normal(key_wave, shape, jnp.float32), -4.0, 4.0)
    scale = jnp.exp(jax.random.uniform(key_scale, (STATIONS, CH, 1), jnp.float32, math.log(0.2), math.log(4.0)))
    envelope = rough_envelope(key_env, (STATIONS, CH), DLEN, 64, 1.0 / 3.0, 3.0)
    return (wave * scale * envelope).astype(jnp.bfloat16)


def draw_templates(key, part):
    key_wave, key_scale, key_env = jax.random.split(key, 3)
    shape = (TEMPLATES, NLIST, CH, TLEN)
    wave = jnp.clip(jax.random.normal(key_wave, shape, jnp.float32), -4.0, 4.0)
    scale = jnp.exp(jax.random.uniform(key_scale, (TEMPLATES, NLIST, CH, 1), jnp.float32, math.log(0.1), math.log(10.0)))
    envelope = rough_envelope(key_env, (TEMPLATES, NLIST, CH), TLEN, 40, 1.0 / 3.0, 3.0)
    return (wave * scale * envelope).astype(jnp.bfloat16)


def draw_station_list(key, part):
    key_hot, key_groups, key_local = jax.random.split(key, 3)
    block_total = GROUPS * TGROUPS
    entries = NLIST * TPL_DEV
    remaining = entries - CAP
    pool_size = (GROUPS - 1) * CAP
    hot_column = jax.random.randint(key_hot, (TGROUPS,), 0, GROUPS).astype(jnp.int32)
    hot_groups = jnp.tile(hot_column, GROUPS)

    def one_block(block_key, hot_group):
        key_pool, key_order = jax.random.split(block_key)
        others = jnp.arange(pool_size, dtype=jnp.int32) // CAP
        others = others + (others >= hot_group).astype(jnp.int32)
        chosen = jax.random.permutation(key_pool, others)[:remaining]
        listed = jnp.concatenate([jnp.full((CAP,), hot_group, jnp.int32), chosen])
        return jax.random.permutation(key_order, listed)
    groups = jax.vmap(one_block)(jax.random.split(key_groups, block_total), hot_groups).reshape(TEMPLATES, NLIST)

    def pick_local(template_key):
        return jax.random.permutation(template_key, STA_GRP)[:NLIST].astype(jnp.int32)
    local_index = jax.vmap(pick_local)(jax.random.split(key_local, TEMPLATES))
    return (groups * STA_GRP + local_index).astype(jnp.int32)


def place_ends(array, own_key, least, high):
    extent = array.shape
    index_at = [jax.random.randint(jax.random.fold_in(own_key, axis), (), 0, extent[axis]) for axis in range(len(extent))]
    array = array.at[tuple(index_at)].set(least)
    longest = extent.index(max(extent))
    index_at[longest] = (index_at[longest] + 1) % extent[longest]
    return array.at[tuple(index_at)].set(high)


def setup_inputs(seed: int = 0) -> dict:
    seeds = jax.random.split(jax.random.key(seed), 5)
    continuous = draw_continuous(jax.random.fold_in(seeds[4], 71), 0)
    templates = draw_templates(jax.random.fold_in(seeds[4], 71), 0)
    station_list = draw_station_list(jax.random.fold_in(seeds[4], 71), 0)
    moveouts = place_ends(jax.random.randint(seeds[3], (TEMPLATES, NLIST), 0, SHIFT_MAX + 1), jax.random.fold_in(seeds[3], 1), 0, SHIFT_MAX).astype(jnp.int32)
    return dict(continuous=continuous, templates=templates, station_list=station_list, moveouts=moveouts)


EPS = 1e-05

def window_inverse(series):
    squares = jnp.square(series.astype(jnp.float32))
    running = jnp.cumsum(squares, axis=-1)
    running = jnp.concatenate([jnp.zeros(running.shape[:-1] + (1,), jnp.float32), running], axis=-1)
    energy = running[..., TLEN:TLEN + OUT] - running[..., :OUT]
    return lax.rsqrt(energy / TLEN + EPS)

def reference(continuous, templates, station_list, moveouts):
    levels = window_inverse(continuous)
    block_size = math.gcd(TEMPLATES, 8)
    block_total = TEMPLATES // block_size

    def one_block(block_parts):
        block_templates, block_list, block_shift = block_parts
        picked_rows = continuous[block_list]
        scales = levels[block_list]
        channel_total = block_size * NLIST * CH
        signals = picked_rows.reshape(1, channel_total, DLEN).astype(jnp.float32)
        kernels = block_templates.reshape(channel_total, 1, TLEN).astype(jnp.float32)
        products = lax.conv_general_dilated(signals, kernels, (1,), 'VALID', feature_group_count=channel_total, precision=lax.Precision.HIGHEST, dimension_numbers=('NCH', 'OIH', 'NCH'))
        products = products[0, :, :OUT].reshape(block_size, NLIST, CH, OUT)
        template_values = block_templates.astype(jnp.float32)
        template_inverse = lax.rsqrt(lax.optimization_barrier(jnp.mean(template_values * template_values, axis=-1)) + EPS)
        normalized = products * scales * (template_inverse / TLEN)[..., None]
        summed = lax.optimization_barrier(jnp.sum(normalized, axis=2))
        slicer = jax.vmap(jax.vmap(lambda series, start_at: lax.dynamic_slice_in_dim(series, start_at, WIN)))
        aligned = slicer(summed, block_shift)
        return lax.optimization_barrier(jnp.sum(aligned, axis=1))
    grouped = (templates.reshape(block_total, block_size, NLIST, CH, TLEN), station_list.reshape(block_total, block_size, NLIST), moveouts.reshape(block_total, block_size, NLIST))
    result = lax.map(one_block, grouped)
    return result.reshape(TEMPLATES, WIN)
```

```python
import jax
import jax.numpy as jnp
from jax import lax
from jax.experimental import pallas as pl
from jax.experimental.pallas import tpu as pltpu
from jax.sharding import PartitionSpec as P

WIN = 768
TLEN = 400
CH = 3
DLEN = 1424
EPS = 1e-05
LANES = 128
TILES = 12
ROWS = 40
CAP = 3
HALF = 64
DEPTH = 512
BLOCKS = WIN // LANES


def prepare(groups, entries, station_ref, data_ref, out_ref, ask_ref, slot_ref, scratch, count):
    list_size = station_ref.shape[1]
    scratch[...] = jnp.zeros_like(scratch)
    for k in range(data_ref.shape[0]):
        x = data_ref[k].astype(jnp.float32)
        for q in range(TILES):
            width = min(LANES, DLEN - q * LANES)
            scratch[pl.ds(k * ROWS + q, CH, stride=TILES), 0:width] = x[
                :, q * LANES : q * LANES + width
            ]
    packed = scratch[...].astype(jnp.bfloat16)
    for d in range(out_ref.shape[0]):
        out_ref[d] = packed
    for g in range(groups):
        count[g] = 0
        for s in range(CAP):
            ask_ref[g, 0, s] = 0
    for e in range(entries):
        station = station_ref[e // list_size, e % list_size]
        g = station // 32
        position = jnp.minimum(count[g], CAP - 1)
        count[g] = position + 1
        ask_ref[g, 0, position] = station - g * 32
        slot_ref[0, e] = g * CAP + position


def build_bands(entries, templates_ref, band_ref, scale_ref, ones_ref, scratch):
    scratch[...] = jnp.zeros_like(scratch)

    def step(e, carry):
        x = templates_ref[e].astype(jnp.float32)
        scratch[0:CH, 0:TLEN] = x
        energy = jnp.sum(x * x, axis=1, keepdims=True)
        scale = lax.rsqrt(energy / TLEN + EPS) / TLEN
        scale_ref[e] = jnp.broadcast_to(scale, (CH, LANES))
        for c in range(CH):
            rows = jnp.broadcast_to(scratch[c : c + 1, :], (HALF, DEPTH))
            band = pltpu.roll(rows, 0, 1, stride=1, stride_axis=0)
            band_ref[c, pl.ds(pl.multiple_of(e * HALF, HALF), HALF), :] = band.astype(jnp.bfloat16)
        return carry

    lax.fori_loop(0, entries, step, 0)
    r = lax.broadcasted_iota(jnp.int32, (LANES, LANES), 0)
    i = lax.broadcasted_iota(jnp.int32, (LANES, LANES), 1)
    kinds = (r >= i, r >= 0, r - i < TLEN - 384, r - i < TLEN - 512)
    for n, kind in enumerate(kinds):
        block = jnp.where(kind, 1.0, 0.0).astype(jnp.bfloat16)
        ones_ref[0:LANES, n * LANES : (n + 1) * LANES] = block
        ones_ref[LANES : 2 * LANES, n * LANES : (n + 1) * LANES] = block


def pick(groups, ask_ref, data_ref, out_ref, sem):
    for i in range(groups):
        for s in range(CAP):
            station = ask_ref[i, 0, s]
            t = station // 2
            k = station - t * 2
            pltpu.make_async_copy(
                data_ref.at[t, pl.ds(pl.multiple_of(k * ROWS, 8), ROWS)],
                out_ref.at[i, pl.ds(s * ROWS, ROWS)],
                sem,
            ).start()
    pltpu.make_async_copy(out_ref, out_ref, sem).wait()


def correlate(
    entries, slot_ref, shift_ref, data_ref, band_ref, scale_ref, ones_ref, out_ref,
    wide, shifted, squares, sums,
):
    groups, rows, _ = data_ref.shape
    list_size = entries // out_ref.shape[0]
    for g in range(groups):
        wide[g * rows : (g + 1) * rows, :] = data_ref[g].astype(jnp.float32)
    wide[groups * rows :, :] = jnp.zeros((wide.shape[0] - groups * rows, LANES), jnp.float32)
    lane = lax.broadcasted_iota(jnp.int32, (ROWS, LANES), 1)
    lane8 = lax.broadcasted_iota(jnp.int32, (8, LANES), 1)
    for e in range(entries):
        shift = shift_ref[e // list_size, e % list_size]
        base = slot_ref[0, e] * ROWS
        for h in range(2):
            moved = shift + h * HALF
            whole = moved // LANES
            part = moved - whole * LANES
            back = jnp.where(part == 0, 0, LANES - part)
            first = pltpu.roll(wide[pl.ds(base + whole, ROWS), :], back, 1)
            second = pltpu.roll(wide[pl.ds(base + whole + 1, ROWS), :], back, 1)
            y = jnp.where(lane < LANES - part, first, second)
            shifted[h, e * ROWS : (e + 1) * ROWS, :] = y
            if h == 0:
                sq = y * y
                high = sq.astype(jnp.bfloat16)
                squares[e * ROWS : (e + 1) * ROWS, 0:LANES] = high
                squares[e * ROWS : (e + 1) * ROWS, LANES:] = (
                    sq - high.astype(jnp.float32)
                ).astype(jnp.bfloat16)
    sums[...] = jnp.dot(squares[...], ones_ref[...], preferred_element_type=jnp.float32)
    totals = [jnp.zeros((8, LANES), jnp.float32) for _ in range(out_ref.shape[0])]
    for quad in range(entries // 4):
        for c in range(CH):
            frames = []
            for n in range(4):
                start = (quad * 4 + n) * ROWS + c * TILES
                for h in range(2):
                    frames.append(
                        jnp.concatenate(
                            [
                                shifted[h, start + q : start + q + 8, :]
                                for q in range(DEPTH // LANES)
                            ],
                            axis=1,
                        )
                    )
            left = jnp.concatenate(frames, axis=0).astype(jnp.bfloat16)
            product = lax.dot_general(
                left,
                band_ref[c, quad * 4 * HALF : (quad + 1) * 4 * HALF, :],
                (((1,), (1,)), ((), ())),
                preferred_element_type=jnp.float32,
            )
            for n in range(4):
                e = quad * 4 + n
                column = (n // 2) * LANES
                low = product[n * 16 : n * 16 + 8, column : column + LANES]
                high = product[n * 16 + 8 : n * 16 + 16, column : column + LANES]
                if n % 2 == 0:
                    high = pltpu.roll(high, HALF, 1)
                else:
                    low = pltpu.roll(low, HALF, 1)
                raw = jnp.where(lane8 < HALF, low, high)
                start = e * ROWS + c * TILES
                energy = (
                    sums[start : start + 8, 0:LANES]
                    + sums[start + 1 : start + 9, LANES : 2 * LANES]
                    + sums[start + 2 : start + 10, LANES : 2 * LANES]
                    + sums[start + 3 : start + 11, 2 * LANES : 3 * LANES]
                    + sums[start + 4 : start + 12, 3 * LANES :]
                )
                level = lax.rsqrt(energy / TLEN + EPS)
                totals[e // list_size] = totals[e // list_size] + raw * level * scale_ref[e][
                    c : c + 1, :
                ]
    for t, total in enumerate(totals):
        for b in range(BLOCKS):
            out_ref[t : t + 1, b * LANES : (b + 1) * LANES] = total[b : b + 1, :]


def shards(continuous, templates, station_list, moveouts):
    groups = lax.axis_size("st")
    peers = lax.axis_size("tp")
    owned = continuous.shape[0]
    template_count, list_size = station_list.shape
    entries = template_count * list_size
    smem = pl.BlockSpec(memory_space=pltpu.SMEM)
    vmem = pl.BlockSpec(memory_space=pltpu.VMEM)
    anywhere = pl.BlockSpec(memory_space=pl.ANY)

    def params():
        return pltpu.CompilerParams(vmem_limit_bytes=48 * 2**20)

    spread, asked, slots = pl.pallas_call(
        lambda *refs: prepare(groups, entries, *refs),
        out_shape=(
            jax.ShapeDtypeStruct((peers, owned * ROWS, LANES), jnp.bfloat16),
            jax.ShapeDtypeStruct((groups, 1, LANES), jnp.int32),
            jax.ShapeDtypeStruct((1, LANES), jnp.int32),
        ),
        in_specs=[smem, vmem],
        out_specs=(vmem, smem, smem),
        scratch_shapes=[
            pltpu.VMEM((owned * ROWS, LANES), jnp.float32),
            pltpu.SMEM((groups,), jnp.int32),
        ],
        compiler_params=params(),
        name="prepare",
    )(station_list, continuous)
    asks = lax.all_to_all(asked, "st", split_axis=0, concat_axis=0, tiled=True)
    group_rows = lax.all_to_all(spread, "tp", split_axis=0, concat_axis=0, tiled=True)
    bands, scales, ones = pl.pallas_call(
        lambda *refs: build_bands(entries, *refs),
        out_shape=(
            jax.ShapeDtypeStruct((CH, entries * HALF, DEPTH), jnp.bfloat16),
            jax.ShapeDtypeStruct((entries, CH, LANES), jnp.float32),
            jax.ShapeDtypeStruct((2 * LANES, 4 * LANES), jnp.bfloat16),
        ),
        in_specs=[vmem],
        out_specs=(vmem, vmem, vmem),
        scratch_shapes=[pltpu.VMEM((8, DEPTH), jnp.float32)],
        compiler_params=params(),
        name="bands",
    )(templates.reshape(entries, CH, TLEN))
    picked = pl.pallas_call(
        lambda *refs: pick(groups, *refs),
        out_shape=jax.ShapeDtypeStruct((groups, CAP * ROWS, LANES), jnp.bfloat16),
        in_specs=[smem, anywhere],
        out_specs=anywhere,
        scratch_shapes=[pltpu.SemaphoreType.DMA],
        compiler_params=params(),
        name="pick",
    )(asks, group_rows)
    records = lax.all_to_all(picked, "st", split_axis=0, concat_axis=0, tiled=True)
    return pl.pallas_call(
        lambda *refs: correlate(entries, *refs),
        out_shape=jax.ShapeDtypeStruct((template_count, WIN), jnp.float32),
        in_specs=[smem, smem, vmem, vmem, vmem, vmem],
        out_specs=vmem,
        scratch_shapes=[
            pltpu.VMEM((groups * CAP * ROWS + 8, LANES), jnp.float32),
            pltpu.VMEM((2, entries * ROWS, LANES), jnp.float32),
            pltpu.VMEM((entries * ROWS, 2 * LANES), jnp.bfloat16),
            pltpu.VMEM((entries * ROWS, 4 * LANES), jnp.float32),
        ],
        compiler_params=params(),
        name="correlate",
    )(slots, moveouts, records, bands, scales, ones)


def solution(mesh):
    placed = (
        P(("st", "tp"), None, None),
        P(("st", "tp"), None, None, None),
        P(("st", "tp"), None),
        P(("st", "tp"), None),
    )
    return jax.shard_map(
        shards, mesh=mesh, in_specs=placed, out_specs=P(("st", "tp"), None), check_vma=False
    )
```

```python
import jax
import jax.numpy as jnp
from jax import lax
from jax.experimental import pallas as pl
from jax.experimental.pallas import tpu as pltpu
from jax.sharding import PartitionSpec as P

WIN = 768
TLEN = 400
CH = 3
DLEN = 1424
EPS = 1e-05
LANES = 128
TILES = 12
ROWS = 40
CAP = 3
HALF = 64
DEPTH = 512
BLOCKS = WIN // LANES


def prepare(
    groups, entries, station_ref, shift_ref, data_ref, out_ref, ask_ref, slot_ref, scratch, count
):
    list_size = station_ref.shape[1]
    owned = data_ref.shape[1]
    scratch[...] = jnp.zeros_like(scratch)
    for c in range(CH):
        x = data_ref[c].astype(jnp.float32)
        for q in range(TILES):
            width = min(LANES, DLEN - q * LANES)
            scratch[pl.ds(c * TILES + q, owned, stride=ROWS), 0:width] = x[
                :, q * LANES : q * LANES + width
            ]
    packed = scratch[...].astype(jnp.bfloat16)
    for d in range(out_ref.shape[0]):
        out_ref[d] = packed
    for g in range(groups):
        count[g] = 0
        for s in range(CAP):
            ask_ref[0, g * CAP + s] = 0
    for e in range(entries):
        station = station_ref[e // list_size, e % list_size]
        g = station // 32
        position = jnp.minimum(count[g], CAP - 1)
        count[g] = position + 1
        ask_ref[0, g * CAP + position] = station - g * 32
        slot_ref[0, e] = g * CAP + position
        slot_ref[1, e] = shift_ref[e // list_size, e % list_size]


def build_bands(entries, templates_ref, band_ref, scale_ref, ones_ref, scratch):
    scratch[...] = jnp.zeros_like(scratch)

    list_size = templates_ref.shape[0]
    owned = templates_ref.shape[2]

    def step(k, carry):
        for c in range(CH):
            x = templates_ref[k, c].astype(jnp.float32)
            scratch[0:owned, 0:TLEN] = x
            energy = jnp.sum(x * x, axis=1, keepdims=True)
            scale = lax.rsqrt(energy / TLEN + EPS) / TLEN
            scale_ref[k, c] = jnp.broadcast_to(scale, (owned, LANES))
            for t in range(owned):
                rows = jnp.broadcast_to(scratch[t : t + 1, :], (HALF, DEPTH))
                band = pltpu.roll(rows, 0, 1, stride=1, stride_axis=0)
                place = pl.multiple_of((t * list_size + k) * HALF, HALF)
                band_ref[c, pl.ds(place, HALF), :] = band.astype(jnp.bfloat16)
        return carry

    lax.fori_loop(0, list_size, step, 0)
    r = lax.broadcasted_iota(jnp.int32, (LANES, LANES), 0)
    i = lax.broadcasted_iota(jnp.int32, (LANES, LANES), 1)
    kinds = (r >= i, r >= 0, r - i < TLEN - 384, r - i < TLEN - 512)
    for n, kind in enumerate(kinds):
        block = jnp.where(kind, 1.0, 0.0).astype(jnp.bfloat16)
        ones_ref[0:LANES, n * LANES : (n + 1) * LANES] = block
        ones_ref[LANES : 2 * LANES, n * LANES : (n + 1) * LANES] = block


def pick(groups, ask_ref, data_ref, out_ref, sem):
    me = lax.axis_index("st")
    for i in range(groups):
        for s in range(CAP):
            station = ask_ref[i, 0, me * CAP + s]
            t = station // 2
            k = station - t * 2
            pltpu.make_async_copy(
                data_ref.at[t, pl.ds(pl.multiple_of(k * ROWS, 8), ROWS)],
                out_ref.at[i, pl.ds(s * ROWS, ROWS)],
                sem,
            ).start()
    pltpu.make_async_copy(out_ref, out_ref, sem).wait()


def correlate(
    entries, slot_ref, data_ref, band_ref, scale_ref, ones_ref, out_ref,
    wide, shifted, squares, sums,
):
    groups, rows, _ = data_ref.shape
    list_size = entries // out_ref.shape[0]
    for g in range(groups):
        wide[g * rows : (g + 1) * rows, :] = data_ref[g].astype(jnp.float32)
    wide[groups * rows :, :] = jnp.zeros((wide.shape[0] - groups * rows, LANES), jnp.float32)
    lane = lax.broadcasted_iota(jnp.int32, (ROWS, LANES), 1)
    lane8 = lax.broadcasted_iota(jnp.int32, (8, LANES), 1)
    for e in range(entries):
        shift = slot_ref[1, e]
        base = slot_ref[0, e] * ROWS
        for h in range(2):
            moved = shift + h * HALF
            whole = moved // LANES
            part = moved - whole * LANES
            back = jnp.where(part == 0, 0, LANES - part)
            first = pltpu.roll(wide[pl.ds(base + whole, ROWS), :], back, 1)
            second = pltpu.roll(wide[pl.ds(base + whole + 1, ROWS), :], back, 1)
            y = jnp.where(lane < LANES - part, first, second)
            shifted[h, e * ROWS : (e + 1) * ROWS, :] = y
            if h == 0:
                sq = y * y
                high = sq.astype(jnp.bfloat16)
                squares[e * ROWS : (e + 1) * ROWS, 0:LANES] = high
                squares[e * ROWS : (e + 1) * ROWS, LANES:] = (
                    sq - high.astype(jnp.float32)
                ).astype(jnp.bfloat16)
    sums[...] = jnp.dot(squares[...], ones_ref[...], preferred_element_type=jnp.float32)
    totals = [jnp.zeros((8, LANES), jnp.float32) for _ in range(out_ref.shape[0])]
    for quad in range(entries // 4):
        for c in range(CH):
            frames = []
            for n in range(4):
                start = (quad * 4 + n) * ROWS + c * TILES
                for h in range(2):
                    frames.append(
                        jnp.concatenate(
                            [
                                shifted[h, start + q : start + q + 8, :]
                                for q in range(DEPTH // LANES)
                            ],
                            axis=1,
                        )
                    )
            left = jnp.concatenate(frames, axis=0).astype(jnp.bfloat16)
            product = lax.dot_general(
                left,
                band_ref[c, quad * 4 * HALF : (quad + 1) * 4 * HALF, :],
                (((1,), (1,)), ((), ())),
                preferred_element_type=jnp.float32,
            )
            for n in range(4):
                e = quad * 4 + n
                column = (n // 2) * LANES
                low = product[n * 16 : n * 16 + 8, column : column + LANES]
                high = product[n * 16 + 8 : n * 16 + 16, column : column + LANES]
                if n % 2 == 0:
                    high = pltpu.roll(high, HALF, 1)
                else:
                    low = pltpu.roll(low, HALF, 1)
                raw = jnp.where(lane8 < HALF, low, high)
                start = e * ROWS + c * TILES
                energy = (
                    sums[start : start + 8, 0:LANES]
                    + sums[start + 1 : start + 9, LANES : 2 * LANES]
                    + sums[start + 2 : start + 10, LANES : 2 * LANES]
                    + sums[start + 3 : start + 11, 2 * LANES : 3 * LANES]
                    + sums[start + 4 : start + 12, 3 * LANES :]
                )
                level = lax.rsqrt(energy / TLEN + EPS)
                totals[e // list_size] = totals[e // list_size] + raw * level * scale_ref[
                    e % list_size, c, e // list_size : e // list_size + 1, :
                ]
    for t, total in enumerate(totals):
        for b in range(BLOCKS):
            out_ref[t : t + 1, b * LANES : (b + 1) * LANES] = total[b : b + 1, :]


def shards(continuous, templates, station_list, moveouts):
    groups = lax.axis_size("st")
    peers = lax.axis_size("tp")
    owned = continuous.shape[0]
    template_count, list_size = station_list.shape
    entries = template_count * list_size
    smem = pl.BlockSpec(memory_space=pltpu.SMEM)
    vmem = pl.BlockSpec(memory_space=pltpu.VMEM)
    anywhere = pl.BlockSpec(memory_space=pl.ANY)

    def params(mebibytes):
        return pltpu.CompilerParams(vmem_limit_bytes=mebibytes * 2**20)

    spread, asked, slots = pl.pallas_call(
        lambda *refs: prepare(groups, entries, *refs),
        out_shape=(
            jax.ShapeDtypeStruct((peers, owned * ROWS, LANES), jnp.bfloat16),
            jax.ShapeDtypeStruct((1, LANES), jnp.int32),
            jax.ShapeDtypeStruct((2, LANES), jnp.int32),
        ),
        in_specs=[smem, smem, vmem],
        out_specs=(vmem, smem, smem),
        scratch_shapes=[
            pltpu.VMEM((owned * ROWS, LANES), jnp.float32),
            pltpu.SMEM((groups,), jnp.int32),
        ],
        compiler_params=params(4),
        name="prepare",
    )(station_list, moveouts, jnp.swapaxes(continuous, 0, 1))
    asks = lax.all_gather(asked, "st", axis=0, tiled=False)
    group_rows = lax.all_to_all(spread, "tp", split_axis=0, concat_axis=0, tiled=True)
    bands, scales, ones = pl.pallas_call(
        lambda *refs: build_bands(entries, *refs),
        out_shape=(
            jax.ShapeDtypeStruct((CH, entries * HALF, DEPTH), jnp.bfloat16),
            jax.ShapeDtypeStruct((list_size, CH, template_count, LANES), jnp.float32),
            jax.ShapeDtypeStruct((2 * LANES, 4 * LANES), jnp.bfloat16),
        ),
        in_specs=[vmem],
        out_specs=(vmem, vmem, vmem),
        scratch_shapes=[pltpu.VMEM((8, DEPTH), jnp.float32)],
        compiler_params=params(12),
        name="bands",
    )(jnp.transpose(templates, (1, 2, 0, 3)))
    picked = pl.pallas_call(
        lambda *refs: pick(groups, *refs),
        out_shape=jax.ShapeDtypeStruct((groups, CAP * ROWS, LANES), jnp.bfloat16),
        in_specs=[smem, anywhere],
        out_specs=anywhere,
        scratch_shapes=[pltpu.SemaphoreType.DMA],
        compiler_params=params(2),
        name="pick",
    )(asks, group_rows)
    records = lax.all_to_all(picked, "st", split_axis=0, concat_axis=0, tiled=True)
    return pl.pallas_call(
        lambda *refs: correlate(entries, *refs),
        out_shape=jax.ShapeDtypeStruct((template_count, WIN), jnp.float32),
        in_specs=[smem, vmem, vmem, vmem, vmem],
        out_specs=vmem,
        scratch_shapes=[
            pltpu.VMEM((groups * CAP * ROWS + 8, LANES), jnp.float32),
            pltpu.VMEM((2, entries * ROWS, LANES), jnp.float32),
            pltpu.VMEM((entries * ROWS, 2 * LANES), jnp.bfloat16),
            pltpu.VMEM((entries * ROWS, 4 * LANES), jnp.float32),
        ],
        compiler_params=params(16),
        name="correlate",
    )(slots, records, bands, scales, ones)


def solution(mesh):
    placed = (
        P(("st", "tp"), None, None),
        P(("st", "tp"), None, None, None),
        P(("st", "tp"), None),
        P(("st", "tp"), None),
    )
    return jax.shard_map(
        shards, mesh=mesh, in_specs=placed, out_specs=P(("st", "tp"), None), check_vma=False
    )
```

```python
import jax
import jax.numpy as jnp
from jax import lax
from jax.experimental import pallas as pl
from jax.experimental.pallas import tpu as pltpu
from jax.sharding import PartitionSpec as P

WIN = 768
TLEN = 400
CH = 3
DLEN = 1424
EPS = 1e-05
LANES = 128
TILES = 12
ROWS = 40
CAP = 3
HALF = 64
DEPTH = 512
BLOCKS = WIN // LANES
SIDE = 4


def rotation(dy, dx):
    return [
        (y * SIDE + x, (y + dy) % SIDE * SIDE + (x + dx) % SIDE)
        for y in range(SIDE)
        for x in range(SIDE)
    ]


def prepare(
    groups, entries, station_ref, shift_ref, data_ref, out_ref, ask_ref, slot_ref, scratch, count
):
    list_size = station_ref.shape[1]
    owned = data_ref.shape[1]
    scratch[...] = jnp.zeros_like(scratch)
    for c in range(CH):
        x = data_ref[c].astype(jnp.float32)
        for q in range(TILES):
            width = min(LANES, DLEN - q * LANES)
            scratch[pl.ds(c * TILES + q, owned, stride=ROWS), 0:width] = x[
                :, q * LANES : q * LANES + width
            ]
    packed = scratch[...].astype(jnp.bfloat16)
    for d in range(out_ref.shape[0]):
        out_ref[d] = packed
    for g in range(groups):
        count[g] = 0
        for s in range(CAP):
            ask_ref[0, g * CAP + s] = 0
    for e in range(entries):
        station = station_ref[e // list_size, e % list_size]
        g = station // 32
        position = jnp.minimum(count[g], CAP - 1)
        count[g] = position + 1
        ask_ref[0, g * CAP + position] = station - g * 32
        slot_ref[0, e] = g * CAP + position
        slot_ref[1, e] = shift_ref[e // list_size, e % list_size]


def build_bands(templates_ref, band_out, scale_ref, ones_ref, scratch, band_ref, sem):
    scratch[...] = jnp.zeros_like(scratch)

    list_size = templates_ref.shape[0]
    owned = templates_ref.shape[2]

    def step(k, carry):
        for c in range(CH):
            x = templates_ref[k, c].astype(jnp.float32)
            scratch[0:owned, 0:TLEN] = x
            energy = jnp.sum(x * x, axis=1, keepdims=True)
            scale = lax.rsqrt(energy / TLEN + EPS) / TLEN
            scale_ref[k, c] = jnp.broadcast_to(scale, (owned, LANES))
            for t in range(owned):
                rows = jnp.broadcast_to(scratch[t : t + 1, :], (HALF, DEPTH))
                band = pltpu.roll(rows, 0, 1, stride=1, stride_axis=0)
                place = pl.multiple_of((t * list_size + k) * HALF, HALF)
                band_ref[c, pl.ds(place, HALF), :] = band.astype(jnp.bfloat16)
                pltpu.make_async_copy(
                    band_ref.at[c, pl.ds(place, HALF)], band_out.at[c, pl.ds(place, HALF)], sem
                ).start()
        return carry

    lax.fori_loop(0, list_size, step, 0)
    r = lax.broadcasted_iota(jnp.int32, (LANES, LANES), 0)
    i = lax.broadcasted_iota(jnp.int32, (LANES, LANES), 1)
    kinds = (r >= i, r >= 0, r - i < TLEN - 384, r - i < TLEN - 512)
    for n, kind in enumerate(kinds):
        block = jnp.where(kind, 1.0, 0.0).astype(jnp.bfloat16)
        ones_ref[0:LANES, n * LANES : (n + 1) * LANES] = block
        ones_ref[LANES : 2 * LANES, n * LANES : (n + 1) * LANES] = block
    pltpu.make_async_copy(band_ref, band_out, sem).wait()


def pick(*refs):
    asks, (data_ref, out_ref, sem) = refs[:SIDE], refs[SIDE:]
    me = lax.axis_index("st")
    y, x = me // SIDE, me % SIDE
    for dy in range(SIDE):
        for dx in range(SIDE):
            i = ((y + SIDE - dy) % SIDE) * SIDE + (x + SIDE - dx) % SIDE
            for s in range(CAP):
                station = asks[dy][dx, me * CAP + s]
                t = station // 2
                k = station - t * 2
                pltpu.make_async_copy(
                    data_ref.at[t, pl.ds(pl.multiple_of(k * ROWS, 8), ROWS)],
                    out_ref.at[i, pl.ds(s * ROWS, ROWS)],
                    sem,
                ).start()
    pltpu.make_async_copy(out_ref, out_ref, sem).wait()


def correlate(
    entries, slot_ref, data_ref, band_in, scale_ref, ones_ref, out_ref,
    wide, shifted, squares, sums, band_ref, sems,
):
    quads = entries // 4
    loads = []
    for quad in range(quads):
        part = pl.ds(quad * 4 * HALF, 4 * HALF)
        loads.append(
            pltpu.make_async_copy(
                band_in.at[:, part], band_ref.at[:, part], sems.at[quad]
            )
        )
        for c in range(CH):
            for n in range(1):
                part = pl.ds(quad * 4 * HALF + n * (4 * HALF // 1), 4 * HALF // 1)
                pltpu.make_async_copy(
                    band_in.at[c, part], band_ref.at[c, part], sems.at[quad]
                ).start()
    groups, rows, _ = data_ref.shape
    list_size = entries // out_ref.shape[0]
    for g in range(groups):
        wide[g * rows : (g + 1) * rows, :] = data_ref[g].astype(jnp.float32)
    wide[groups * rows :, :] = jnp.zeros((wide.shape[0] - groups * rows, LANES), jnp.float32)
    lane = lax.broadcasted_iota(jnp.int32, (ROWS, LANES), 1)
    lane8 = lax.broadcasted_iota(jnp.int32, (8, LANES), 1)
    for e in range(entries):
        shift = slot_ref[1, e]
        base = slot_ref[0, e] * ROWS
        for h in range(2):
            moved = shift + h * HALF
            whole = moved // LANES
            part = moved - whole * LANES
            back = jnp.where(part == 0, 0, LANES - part)
            first = pltpu.roll(wide[pl.ds(base + whole, ROWS), :], back, 1)
            second = pltpu.roll(wide[pl.ds(base + whole + 1, ROWS), :], back, 1)
            y = jnp.where(lane < LANES - part, first, second)
            shifted[h, e * ROWS : (e + 1) * ROWS, :] = y
            if h == 0:
                sq = y * y
                high = sq.astype(jnp.bfloat16)
                squares[e * ROWS : (e + 1) * ROWS, 0:LANES] = high
                squares[e * ROWS : (e + 1) * ROWS, LANES:] = (
                    sq - high.astype(jnp.float32)
                ).astype(jnp.bfloat16)
    sums[...] = jnp.dot(squares[...], ones_ref[...], preferred_element_type=jnp.float32)
    totals = [jnp.zeros((8, LANES), jnp.float32) for _ in range(out_ref.shape[0])]
    for quad in range(quads):
        loads[quad].wait()
        for c in range(CH):
            frames = []
            for n in range(4):
                start = (quad * 4 + n) * ROWS + c * TILES
                for h in range(2):
                    frames.append(
                        jnp.concatenate(
                            [
                                shifted[h, start + q : start + q + 8, :]
                                for q in range(DEPTH // LANES)
                            ],
                            axis=1,
                        )
                    )
            left = jnp.concatenate(frames, axis=0).astype(jnp.bfloat16)
            product = lax.dot_general(
                left,
                band_ref[c, quad * 4 * HALF : (quad + 1) * 4 * HALF, :],
                (((1,), (1,)), ((), ())),
                preferred_element_type=jnp.float32,
            )
            for n in range(4):
                e = quad * 4 + n
                column = (n // 2) * LANES
                low = product[n * 16 : n * 16 + 8, column : column + LANES]
                high = product[n * 16 + 8 : n * 16 + 16, column : column + LANES]
                if n % 2 == 0:
                    high = pltpu.roll(high, HALF, 1)
                else:
                    low = pltpu.roll(low, HALF, 1)
                raw = jnp.where(lane8 < HALF, low, high)
                start = e * ROWS + c * TILES
                energy = (
                    sums[start : start + 8, 0:LANES]
                    + sums[start + 1 : start + 9, LANES : 2 * LANES]
                    + sums[start + 2 : start + 10, LANES : 2 * LANES]
                    + sums[start + 3 : start + 11, 2 * LANES : 3 * LANES]
                    + sums[start + 4 : start + 12, 3 * LANES :]
                )
                level = lax.rsqrt(energy / TLEN + EPS)
                totals[e // list_size] = totals[e // list_size] + raw * level * scale_ref[
                    e % list_size, c, e // list_size : e // list_size + 1, :
                ]
    for t, total in enumerate(totals):
        for b in range(BLOCKS):
            out_ref[t : t + 1, b * LANES : (b + 1) * LANES] = total[b : b + 1, :]


def shards(continuous, templates, station_list, moveouts):
    groups = lax.axis_size("st")
    peers = lax.axis_size("tp")
    owned = continuous.shape[0]
    template_count, list_size = station_list.shape
    entries = template_count * list_size
    smem = pl.BlockSpec(memory_space=pltpu.SMEM)
    vmem = pl.BlockSpec(memory_space=pltpu.VMEM)
    anywhere = pl.BlockSpec(memory_space=pl.ANY)
    hbm = pl.BlockSpec(memory_space=pltpu.HBM)

    def from_hbm(array):
        return pltpu.with_memory_space_constraint(array, pltpu.HBM)

    def params(mebibytes):
        return pltpu.CompilerParams(vmem_limit_bytes=mebibytes * 2**20)

    spread, asked, slots = pl.pallas_call(
        lambda *refs: prepare(groups, entries, *refs),
        out_shape=(
            jax.ShapeDtypeStruct((peers, owned * ROWS, LANES), jnp.bfloat16),
            jax.ShapeDtypeStruct((1, LANES), jnp.int32),
            jax.ShapeDtypeStruct((2, LANES), jnp.int32),
        ),
        in_specs=[smem, smem, vmem],
        out_specs=(vmem, smem, smem),
        scratch_shapes=[
            pltpu.VMEM((owned * ROWS, LANES), jnp.float32),
            pltpu.SMEM((groups,), jnp.int32),
        ],
        compiler_params=params(4),
        name="prepare",
    )(from_hbm(station_list), from_hbm(moveouts), from_hbm(jnp.swapaxes(continuous, 0, 1)))
    along_x = [asked] + [lax.ppermute(asked, "st", rotation(0, d)) for d in range(1, SIDE)]
    row = jnp.concatenate(along_x, axis=0)
    asks = [row] + [lax.ppermute(row, "st", rotation(d, 0)) for d in range(1, SIDE)]
    group_rows = lax.all_to_all(spread, "tp", split_axis=0, concat_axis=0, tiled=True)
    bands, scales, ones = pl.pallas_call(
        build_bands,
        out_shape=(
            pltpu.HBM((CH, entries * HALF, DEPTH), jnp.bfloat16),
            jax.ShapeDtypeStruct((list_size, CH, template_count, LANES), jnp.float32),
            jax.ShapeDtypeStruct((2 * LANES, 4 * LANES), jnp.bfloat16),
        ),
        in_specs=[vmem],
        out_specs=(hbm, vmem, vmem),
        scratch_shapes=[
            pltpu.VMEM((8, DEPTH), jnp.float32),
            pltpu.VMEM((CH, entries * HALF, DEPTH), jnp.bfloat16),
            pltpu.SemaphoreType.DMA,
        ],
        compiler_params=params(12),
        name="bands",
    )(from_hbm(jnp.transpose(templates, (1, 2, 0, 3))))
    picked = pl.pallas_call(
        pick,
        out_shape=jax.ShapeDtypeStruct((groups, CAP * ROWS, LANES), jnp.bfloat16),
        in_specs=[smem] * SIDE + [anywhere],
        out_specs=anywhere,
        scratch_shapes=[pltpu.SemaphoreType.DMA],
        compiler_params=params(2),
        name="pick",
    )(*asks, group_rows)
    records = lax.all_to_all(picked, "st", split_axis=0, concat_axis=0, tiled=True)
    return pl.pallas_call(
        lambda *refs: correlate(entries, *refs),
        out_shape=jax.ShapeDtypeStruct((template_count, WIN), jnp.float32),
        in_specs=[smem, vmem, hbm, vmem, vmem],
        out_specs=vmem,
        scratch_shapes=[
            pltpu.VMEM((groups * CAP * ROWS + 8, LANES), jnp.float32),
            pltpu.VMEM((2, entries * ROWS, LANES), jnp.float32),
            pltpu.VMEM((entries * ROWS, 2 * LANES), jnp.bfloat16),
            pltpu.VMEM((entries * ROWS, 4 * LANES), jnp.float32),
            pltpu.VMEM((CH, entries * HALF, DEPTH), jnp.bfloat16),
            pltpu.SemaphoreType.DMA((entries // 4,)),
        ],
        compiler_params=params(16),
        name="correlate",
    )(slots, records, from_hbm(bands), scales, ones)


def solution(mesh):
    placed = (
        P(("st", "tp"), None, None),
        P(("st", "tp"), None, None, None),
        P(("st", "tp"), None),
        P(("st", "tp"), None),
    )
    return jax.shard_map(
        shards, mesh=mesh, in_specs=placed, out_specs=P(("st", "tp"), None), check_vma=False
    )
```

```python
import jax
import jax.numpy as jnp
from jax import lax
from jax.experimental import pallas as pl
from jax.experimental.pallas import tpu as pltpu
from jax.sharding import PartitionSpec as P

WIN = 768
TLEN = 400
CH = 3
DLEN = 1424
EPS = 1e-05
LANES = 128
TILES = 12
ROWS = 40
CAP = 3
PITCH = 48
STEP = 32
PHASES = LANES // STEP
DEPTH = 512
BLOCKS = WIN // LANES
SIDE = 4


def rotation(dy, dx):
    return [
        (y * SIDE + x, (y + dy) % SIDE * SIDE + (x + dx) % SIDE)
        for y in range(SIDE)
        for x in range(SIDE)
    ]


def prepare(
    groups, entries, station_ref, shift_ref, data_ref, out_ref, ask_ref, slot_ref, scratch, count
):
    list_size = station_ref.shape[1]
    owned = data_ref.shape[1]
    scratch[...] = jnp.zeros_like(scratch)
    for c in range(CH):
        x = data_ref[c].astype(jnp.float32)
        for q in range(TILES):
            width = min(LANES, DLEN - q * LANES)
            scratch[pl.ds(c * TILES + q, owned, stride=ROWS), 0:width] = x[
                :, q * LANES : q * LANES + width
            ]
    packed = scratch[...].astype(jnp.bfloat16)
    for d in range(out_ref.shape[0]):
        out_ref[d] = packed
    for g in range(groups):
        count[g] = 0
        for s in range(CAP):
            ask_ref[0, g * CAP + s] = 0
    for e in range(entries):
        station = station_ref[e // list_size, e % list_size]
        g = station // 32
        position = jnp.minimum(count[g], CAP - 1)
        count[g] = position + 1
        ask_ref[0, g * CAP + position] = station - g * 32
        slot_ref[0, e] = g * CAP + position
        slot_ref[1, e] = shift_ref[e // list_size, e % list_size]


def build_bands(shift_ref, templates_ref, band_ref, scale_ref, ones_ref, scratch):
    scratch[...] = jnp.zeros_like(scratch)
    list_size = templates_ref.shape[0]
    owned = templates_ref.shape[2]

    def step(k, carry):
        for c in range(CH):
            x = templates_ref[k, c].astype(jnp.float32)
            scratch[0:owned, 0:TLEN] = x
            energy = jnp.sum(x * x, axis=1, keepdims=True)
            scale = lax.rsqrt(energy / TLEN + EPS) / TLEN
            scale_ref[k, c] = jnp.broadcast_to(scale, (owned, LANES))
            for t in range(owned):
                moved = pltpu.roll(scratch[...], shift_ref[t, k] % STEP, 1)
                rows = jnp.broadcast_to(moved[t : t + 1, :], (STEP, DEPTH))
                band = pltpu.roll(rows, 0, 1, stride=1, stride_axis=0)
                place = pl.multiple_of((t * list_size + k) * STEP, STEP)
                band_ref[c, pl.ds(place, STEP), :] = band.astype(jnp.bfloat16)
        return carry

    lax.fori_loop(0, list_size, step, 0)
    r = lax.broadcasted_iota(jnp.int32, (LANES, LANES), 0)
    i = lax.broadcasted_iota(jnp.int32, (LANES, LANES), 1)
    kinds = (r >= i, r >= 0, r - i < TLEN - 384, r - i < TLEN - 512)
    for n, kind in enumerate(kinds):
        block = jnp.where(kind, 1.0, 0.0).astype(jnp.bfloat16)
        ones_ref[0:LANES, n * LANES : (n + 1) * LANES] = block
        ones_ref[LANES : 2 * LANES, n * LANES : (n + 1) * LANES] = block


def pick(*refs):
    asks, (data_ref, out_ref, sem) = refs[:SIDE], refs[SIDE:]
    me = lax.axis_index("st")
    y, x = me // SIDE, me % SIDE
    for dy in range(SIDE):
        for dx in range(SIDE):
            i = ((y + SIDE - dy) % SIDE) * SIDE + (x + SIDE - dx) % SIDE
            for s in range(CAP):
                station = asks[dy][dx, me * CAP + s]
                t = station // 2
                k = station - t * 2
                pltpu.make_async_copy(
                    data_ref.at[t, pl.ds(pl.multiple_of(k * ROWS, 8), ROWS)],
                    out_ref.at[i, pl.ds(s * ROWS, ROWS)],
                    sem,
                ).start()
    pltpu.make_async_copy(out_ref, out_ref, sem).wait()


def correlate(
    entries, slot_ref, data_ref, band_ref, scale_ref, ones_ref, out_ref,
    wide, turned, versions, squares, sums,
):
    groups, rows, _ = data_ref.shape
    list_size = entries // out_ref.shape[0]
    for g in range(groups):
        wide[g * rows : (g + 1) * rows, :] = data_ref[g].astype(jnp.float32)
    wide[groups * rows :, :] = jnp.zeros((wide.shape[0] - groups * rows, LANES), jnp.float32)
    lane = lax.broadcasted_iota(jnp.int32, (ROWS, LANES), 1)
    lane8 = lax.broadcasted_iota(jnp.int32, (8, LANES), 1)
    for e in range(entries):
        shift = slot_ref[1, e]
        base = pl.multiple_of(slot_ref[0, e] * ROWS, 8)
        whole = shift // LANES
        part = shift - whole * LANES
        back = jnp.where(part == 0, 0, LANES - part)
        first = pltpu.roll(wide[pl.ds(base + whole, ROWS), :], back, 1)
        second = pltpu.roll(wide[pl.ds(base + whole + 1, ROWS), :], back, 1)
        y = jnp.where(lane < LANES - part, first, second)
        sq = y * y
        high = sq.astype(jnp.bfloat16)
        squares[e * ROWS : (e + 1) * ROWS, 0:LANES] = high
        squares[e * ROWS : (e + 1) * ROWS, LANES:] = (sq - high.astype(jnp.float32)).astype(
            jnp.bfloat16
        )
        record = wide[pl.ds(base, ROWS), :]
        start = e * PITCH
        versions[0, start : start + ROWS, :] = record
        for k in range(1, PHASES):
            moved = pltpu.roll(record, LANES - k * STEP, 1)
            turned[k - 1, start : start + ROWS, :] = moved
            versions[k, start : start + ROWS, :] = jnp.where(
                lane < LANES - k * STEP, moved, turned[k - 1, start + 1 : start + 1 + ROWS, :]
            )
    sums[...] = jnp.dot(squares[...], ones_ref[...], preferred_element_type=jnp.float32)
    totals = [jnp.zeros((8, LANES), jnp.float32) for _ in range(out_ref.shape[0])]
    for batch in range(entries // 8):
        for c in range(CH):
            frames = []
            for n in range(8):
                e = batch * 8 + n
                coarse = slot_ref[1, e] // STEP
                for h in range(PHASES):
                    at = coarse + h
                    version = at % PHASES
                    start = e * PITCH + c * TILES + at // PHASES
                    frames.append(
                        jnp.concatenate(
                            [
                                versions[version, pl.ds(start + q, 8), :]
                                for q in range(DEPTH // LANES)
                            ],
                            axis=1,
                        )
                    )
            left = jnp.concatenate(frames, axis=0).astype(jnp.bfloat16)
            product = lax.dot_general(
                left,
                band_ref[c, batch * 8 * STEP : (batch + 1) * 8 * STEP, :],
                (((1,), (1,)), ((), ())),
                preferred_element_type=jnp.float32,
            )
            for n in range(8):
                e = batch * 8 + n
                column = (n // PHASES) * LANES
                raw = None
                for h in range(PHASES):
                    piece = product[
                        (n * PHASES + h) * 8 : (n * PHASES + h + 1) * 8, column : column + LANES
                    ]
                    turn = (h - n) % PHASES * STEP
                    if turn:
                        piece = pltpu.roll(piece, turn, 1)
                    raw = piece if raw is None else jnp.where(lane8 < h * STEP, raw, piece)
                start = e * ROWS + c * TILES
                energy = (
                    sums[start : start + 8, 0:LANES]
                    + sums[start + 1 : start + 9, LANES : 2 * LANES]
                    + sums[start + 2 : start + 10, LANES : 2 * LANES]
                    + sums[start + 3 : start + 11, 2 * LANES : 3 * LANES]
                    + sums[start + 4 : start + 12, 3 * LANES :]
                )
                level = lax.rsqrt(energy / TLEN + EPS)
                totals[e // list_size] = totals[e // list_size] + raw * level * scale_ref[
                    e % list_size, c, e // list_size : e // list_size + 1, :
                ]
    for t, total in enumerate(totals):
        for b in range(BLOCKS):
            out_ref[t : t + 1, b * LANES : (b + 1) * LANES] = total[b : b + 1, :]


def shards(continuous, templates, station_list, moveouts):
    groups = lax.axis_size("st")
    peers = lax.axis_size("tp")
    owned = continuous.shape[0]
    template_count, list_size = station_list.shape
    entries = template_count * list_size
    smem = pl.BlockSpec(memory_space=pltpu.SMEM)
    vmem = pl.BlockSpec(memory_space=pltpu.VMEM)
    anywhere = pl.BlockSpec(memory_space=pl.ANY)

    def from_hbm(array):
        return pltpu.with_memory_space_constraint(array, pltpu.HBM)

    def params(mebibytes):
        return pltpu.CompilerParams(vmem_limit_bytes=mebibytes * 2**20)

    spread, asked, slots = pl.pallas_call(
        lambda *refs: prepare(groups, entries, *refs),
        out_shape=(
            jax.ShapeDtypeStruct((peers, owned * ROWS, LANES), jnp.bfloat16),
            jax.ShapeDtypeStruct((1, LANES), jnp.int32),
            jax.ShapeDtypeStruct((2, LANES), jnp.int32),
        ),
        in_specs=[smem, smem, vmem],
        out_specs=(vmem, smem, smem),
        scratch_shapes=[
            pltpu.VMEM((owned * ROWS, LANES), jnp.float32),
            pltpu.SMEM((groups,), jnp.int32),
        ],
        compiler_params=params(4),
        name="prepare",
    )(from_hbm(station_list), from_hbm(moveouts), from_hbm(jnp.swapaxes(continuous, 0, 1)))
    along_x = [asked] + [lax.ppermute(asked, "st", rotation(0, d)) for d in range(1, SIDE)]
    row = jnp.concatenate(along_x, axis=0)
    asks = [row] + [lax.ppermute(row, "st", rotation(d, 0)) for d in range(1, SIDE)]
    group_rows = lax.all_to_all(spread, "tp", split_axis=0, concat_axis=0, tiled=True)
    bands, scales, ones = pl.pallas_call(
        build_bands,
        out_shape=(
            jax.ShapeDtypeStruct((CH, entries * STEP, DEPTH), jnp.bfloat16),
            jax.ShapeDtypeStruct((list_size, CH, template_count, LANES), jnp.float32),
            jax.ShapeDtypeStruct((2 * LANES, 4 * LANES), jnp.bfloat16),
        ),
        in_specs=[smem, vmem],
        out_specs=(vmem, vmem, vmem),
        scratch_shapes=[pltpu.VMEM((8, DEPTH), jnp.float32)],
        compiler_params=params(12),
        name="bands",
    )(from_hbm(moveouts), from_hbm(jnp.transpose(templates, (1, 2, 0, 3))))
    picked = pl.pallas_call(
        pick,
        out_shape=jax.ShapeDtypeStruct((groups, CAP * ROWS, LANES), jnp.bfloat16),
        in_specs=[smem] * SIDE + [anywhere],
        out_specs=anywhere,
        scratch_shapes=[pltpu.SemaphoreType.DMA],
        compiler_params=params(2),
        name="pick",
    )(*asks, group_rows)
    records = lax.all_to_all(picked, "st", split_axis=0, concat_axis=0, tiled=True)
    return pl.pallas_call(
        lambda *refs: correlate(entries, *refs),
        out_shape=jax.ShapeDtypeStruct((template_count, WIN), jnp.float32),
        in_specs=[smem, vmem, vmem, vmem, vmem],
        out_specs=vmem,
        scratch_shapes=[
            pltpu.VMEM((groups * CAP * ROWS + 8, LANES), jnp.float32),
            pltpu.VMEM((PHASES - 1, entries * PITCH, LANES), jnp.float32),
            pltpu.VMEM((PHASES, entries * PITCH, LANES), jnp.float32),
            pltpu.VMEM((entries * ROWS, 2 * LANES), jnp.bfloat16),
            pltpu.VMEM((entries * ROWS, 4 * LANES), jnp.float32),
        ],
        compiler_params=params(20),
        name="correlate",
    )(slots, records, bands, scales, ones)


def solution(mesh):
    placed = (
        P(("st", "tp"), None, None),
        P(("st", "tp"), None, None, None),
        P(("st", "tp"), None),
        P(("st", "tp"), None),
    )
    return jax.shard_map(
        shards, mesh=mesh, in_specs=placed, out_specs=P(("st", "tp"), None), check_vma=False
    )
```

```python
import jax
import jax.numpy as jnp
from jax import lax
from jax.experimental import pallas as pl
from jax.experimental.pallas import tpu as pltpu
from jax.sharding import PartitionSpec as P

WIN = 768
TLEN = 400
CH = 3
DLEN = 1424
EPS = 1e-05
LANES = 128
TILES = 12
ROWS = 40
CAP = 3
PITCH = 48
STEP = 32
PHASES = LANES // STEP
DEPTH = 512
BLOCKS = WIN // LANES
SIDE = 4


def rotation(dy, dx):
    return [
        (y * SIDE + x, (y + dy) % SIDE * SIDE + (x + dx) % SIDE)
        for y in range(SIDE)
        for x in range(SIDE)
    ]


def prepare(
    groups, entries, station_ref, shift_ref, data_ref, out_ref, ask_ref, slot_ref, scratch, count
):
    list_size = station_ref.shape[1]
    owned = data_ref.shape[1]
    scratch[...] = jnp.zeros_like(scratch)
    for c in range(CH):
        x = data_ref[c].astype(jnp.float32)
        for q in range(TILES):
            width = min(LANES, DLEN - q * LANES)
            scratch[pl.ds(c * TILES + q, owned, stride=ROWS), 0:width] = x[
                :, q * LANES : q * LANES + width
            ]
    packed = scratch[...].astype(jnp.bfloat16)
    for d in range(out_ref.shape[0]):
        out_ref[d] = packed
    for g in range(groups):
        count[g] = 0
        for s in range(CAP):
            ask_ref[0, g * CAP + s] = 0
    for e in range(entries):
        station = station_ref[e // list_size, e % list_size]
        g = station // 32
        position = jnp.minimum(count[g], CAP - 1)
        count[g] = position + 1
        ask_ref[0, g * CAP + position] = station - g * 32
        slot_ref[0, e] = g * CAP + position
        slot_ref[1, e] = shift_ref[e // list_size, e % list_size]


def build_bands(shift_ref, templates_ref, band_ref, scale_ref, ones_ref, scratch):
    scratch[...] = jnp.zeros_like(scratch)
    list_size = templates_ref.shape[0]
    owned = templates_ref.shape[2]

    def step(k, carry):
        for c in range(CH):
            x = templates_ref[k, c].astype(jnp.float32)
            scratch[0:owned, 0:TLEN] = x
            energy = jnp.sum(x * x, axis=1, keepdims=True)
            scale = lax.rsqrt(energy / TLEN + EPS) / TLEN
            scale_ref[k, c] = jnp.broadcast_to(scale, (owned, LANES))
            for t in range(owned):
                moved = pltpu.roll(scratch[...], shift_ref[t, k] % STEP, 1)
                rows = jnp.broadcast_to(moved[t : t + 1, :], (STEP, DEPTH))
                band = pltpu.roll(rows, 0, 1, stride=1, stride_axis=0)
                place = pl.multiple_of((t * list_size + k) * STEP, STEP)
                band_ref[c, pl.ds(place, STEP), :] = band.astype(jnp.bfloat16)
        return carry

    lax.fori_loop(0, list_size, step, 0)
    r = lax.broadcasted_iota(jnp.int32, (LANES, LANES), 0)
    i = lax.broadcasted_iota(jnp.int32, (LANES, LANES), 1)
    kinds = (r >= i, r >= 0, r - i < TLEN - 384, r - i < TLEN - 512)
    for n, kind in enumerate(kinds):
        block = jnp.where(kind, 1.0, 0.0).astype(jnp.bfloat16)
        ones_ref[0:LANES, n * LANES : (n + 1) * LANES] = block
        ones_ref[LANES : 2 * LANES, n * LANES : (n + 1) * LANES] = block


def pick(*refs):
    asks, (data_ref, out_ref, sem) = refs[:SIDE], refs[SIDE:]
    me = lax.axis_index("st")
    y, x = me // SIDE, me % SIDE
    for dy in range(SIDE):
        for dx in range(SIDE):
            i = ((y + SIDE - dy) % SIDE) * SIDE + (x + SIDE - dx) % SIDE
            for s in range(CAP):
                station = asks[dy][dx, me * CAP + s]
                t = station // 2
                k = station - t * 2
                pltpu.make_async_copy(
                    data_ref.at[t, pl.ds(pl.multiple_of(k * ROWS, 8), ROWS)],
                    out_ref.at[i, pl.ds(s * ROWS, ROWS)],
                    sem,
                ).start()
    pltpu.make_async_copy(out_ref, out_ref, sem).wait()


def correlate(
    entries, slot_ref, data_ref, band_ref, scale_ref, ones_ref, out_ref,
    wide, turned, versions, squares, sums,
):
    list_size = entries // out_ref.shape[0]
    lane = lax.broadcasted_iota(jnp.int32, (ROWS, LANES), 1)
    lane8 = lax.broadcasted_iota(jnp.int32, (8, LANES), 1)
    totals = [jnp.zeros((8, LANES), jnp.float32) for _ in range(out_ref.shape[0])]
    for batch in range(entries // 8):
        for e in range(batch * 8, batch * 8 + 8):
            shift = slot_ref[1, e]
            slot = slot_ref[0, e]
            group = slot // CAP
            row = pl.multiple_of((slot - group * CAP) * ROWS, 8)
            record = data_ref[group, pl.ds(row, ROWS), :].astype(jnp.float32)
            base = e * PITCH
            wide[base : base + ROWS, :] = record
            wide[base + ROWS : base + PITCH, :] = jnp.zeros((PITCH - ROWS, LANES), jnp.float32)
            whole = shift // LANES
            part = shift - whole * LANES
            back = jnp.where(part == 0, 0, LANES - part)
            first = pltpu.roll(wide[pl.ds(base + whole, ROWS), :], back, 1)
            second = pltpu.roll(wide[pl.ds(base + whole + 1, ROWS), :], back, 1)
            y = jnp.where(lane < LANES - part, first, second)
            sq = y * y
            high = sq.astype(jnp.bfloat16)
            squares[e * ROWS : (e + 1) * ROWS, 0:LANES] = high
            squares[e * ROWS : (e + 1) * ROWS, LANES:] = (sq - high.astype(jnp.float32)).astype(
                jnp.bfloat16
            )
            start = e * PITCH
            versions[0, start : start + ROWS, :] = record
            for k in range(1, PHASES):
                moved = pltpu.roll(record, LANES - k * STEP, 1)
                turned[k - 1, start : start + ROWS, :] = moved
                versions[k, start : start + ROWS, :] = jnp.where(
                    lane < LANES - k * STEP, moved, turned[k - 1, start + 1 : start + 1 + ROWS, :]
                )
        part = slice(batch * 8 * ROWS, (batch + 1) * 8 * ROWS)
        sums[part, :] = jnp.dot(
            squares[part, :], ones_ref[...], preferred_element_type=jnp.float32
        )
        for c in range(CH):
            frames = []
            for n in range(8):
                e = batch * 8 + n
                coarse = slot_ref[1, e] // STEP
                for h in range(PHASES):
                    at = coarse + h
                    version = at % PHASES
                    start = e * PITCH + c * TILES + at // PHASES
                    frames.append(
                        jnp.concatenate(
                            [
                                versions[version, pl.ds(start + q, 8), :]
                                for q in range(DEPTH // LANES)
                            ],
                            axis=1,
                        )
                    )
            left = jnp.concatenate(frames, axis=0).astype(jnp.bfloat16)
            product = lax.dot_general(
                left,
                band_ref[c, batch * 8 * STEP : (batch + 1) * 8 * STEP, :],
                (((1,), (1,)), ((), ())),
                preferred_element_type=jnp.float32,
            )
            for n in range(8):
                e = batch * 8 + n
                column = (n // PHASES) * LANES
                raw = None
                for h in range(PHASES):
                    piece = product[
                        (n * PHASES + h) * 8 : (n * PHASES + h + 1) * 8, column : column + LANES
                    ]
                    turn = (h - n) % PHASES * STEP
                    if turn:
                        piece = pltpu.roll(piece, turn, 1)
                    raw = piece if raw is None else jnp.where(lane8 < h * STEP, raw, piece)
                start = e * ROWS + c * TILES
                energy = (
                    sums[start : start + 8, 0:LANES]
                    + sums[start + 1 : start + 9, LANES : 2 * LANES]
                    + sums[start + 2 : start + 10, LANES : 2 * LANES]
                    + sums[start + 3 : start + 11, 2 * LANES : 3 * LANES]
                    + sums[start + 4 : start + 12, 3 * LANES :]
                )
                level = lax.rsqrt(energy / TLEN + EPS)
                totals[e // list_size] = totals[e // list_size] + raw * level * scale_ref[
                    e % list_size, c, e // list_size : e // list_size + 1, :
                ]
    for t, total in enumerate(totals):
        for b in range(BLOCKS):
            out_ref[t : t + 1, b * LANES : (b + 1) * LANES] = total[b : b + 1, :]


def shards(continuous, templates, station_list, moveouts):
    groups = lax.axis_size("st")
    peers = lax.axis_size("tp")
    owned = continuous.shape[0]
    template_count, list_size = station_list.shape
    entries = template_count * list_size
    smem = pl.BlockSpec(memory_space=pltpu.SMEM)
    vmem = pl.BlockSpec(memory_space=pltpu.VMEM)
    anywhere = pl.BlockSpec(memory_space=pl.ANY)

    def from_hbm(array):
        return pltpu.with_memory_space_constraint(array, pltpu.HBM)

    def params(mebibytes):
        return pltpu.CompilerParams(vmem_limit_bytes=mebibytes * 2**20)

    spread, asked, slots = pl.pallas_call(
        lambda *refs: prepare(groups, entries, *refs),
        out_shape=(
            jax.ShapeDtypeStruct((peers, owned * ROWS, LANES), jnp.bfloat16),
            jax.ShapeDtypeStruct((1, LANES), jnp.int32),
            jax.ShapeDtypeStruct((2, LANES), jnp.int32),
        ),
        in_specs=[smem, smem, vmem],
        out_specs=(vmem, smem, smem),
        scratch_shapes=[
            pltpu.VMEM((owned * ROWS, LANES), jnp.float32),
            pltpu.SMEM((groups,), jnp.int32),
        ],
        compiler_params=params(4),
        name="prepare",
    )(from_hbm(station_list), from_hbm(moveouts), from_hbm(jnp.swapaxes(continuous, 0, 1)))
    along_x = [asked] + [lax.ppermute(asked, "st", rotation(0, d)) for d in range(1, SIDE)]
    row = jnp.concatenate(along_x, axis=0)
    asks = [row] + [lax.ppermute(row, "st", rotation(d, 0)) for d in range(1, SIDE)]
    group_rows = lax.all_to_all(spread, "tp", split_axis=0, concat_axis=0, tiled=True)
    bands, scales, ones = pl.pallas_call(
        build_bands,
        out_shape=(
            jax.ShapeDtypeStruct((CH, entries * STEP, DEPTH), jnp.bfloat16),
            jax.ShapeDtypeStruct((list_size, CH, template_count, LANES), jnp.float32),
            jax.ShapeDtypeStruct((2 * LANES, 4 * LANES), jnp.bfloat16),
        ),
        in_specs=[smem, vmem],
        out_specs=(vmem, vmem, vmem),
        scratch_shapes=[pltpu.VMEM((8, DEPTH), jnp.float32)],
        compiler_params=params(12),
        name="bands",
    )(from_hbm(moveouts), from_hbm(jnp.transpose(templates, (1, 2, 0, 3))))
    picked = pl.pallas_call(
        pick,
        out_shape=jax.ShapeDtypeStruct((groups, CAP * ROWS, LANES), jnp.bfloat16),
        in_specs=[smem] * SIDE + [anywhere],
        out_specs=anywhere,
        scratch_shapes=[pltpu.SemaphoreType.DMA],
        compiler_params=params(2),
        name="pick",
    )(*asks, group_rows)
    records = lax.all_to_all(picked, "st", split_axis=0, concat_axis=0, tiled=True)
    return pl.pallas_call(
        lambda *refs: correlate(entries, *refs),
        out_shape=jax.ShapeDtypeStruct((template_count, WIN), jnp.float32),
        in_specs=[smem, vmem, vmem, vmem, vmem],
        out_specs=vmem,
        scratch_shapes=[
            pltpu.VMEM((entries * PITCH, LANES), jnp.float32),
            pltpu.VMEM((PHASES - 1, entries * PITCH, LANES), jnp.float32),
            pltpu.VMEM((PHASES, entries * PITCH, LANES), jnp.float32),
            pltpu.VMEM((entries * ROWS, 2 * LANES), jnp.bfloat16),
            pltpu.VMEM((entries * ROWS, 4 * LANES), jnp.float32),
        ],
        compiler_params=params(20),
        name="correlate",
    )(slots, records, bands, scales, ones)


def solution(mesh):
    placed = (
        P(("st", "tp"), None, None),
        P(("st", "tp"), None, None, None),
        P(("st", "tp"), None),
        P(("st", "tp"), None),
    )
    return jax.shard_map(
        shards, mesh=mesh, in_specs=placed, out_specs=P(("st", "tp"), None), check_vma=False
    )
```

```python
import jax
import jax.numpy as jnp
from jax import lax
from jax.experimental import pallas as pl
from jax.experimental.pallas import tpu as pltpu
from jax.sharding import PartitionSpec as P

WIN = 768
TLEN = 400
CH = 3
DLEN = 1424
EPS = 1e-05
LANES = 128
TILES = 12
ROWS = 40
CAP = 3
PITCH = 48
STEP = 32
PHASES = LANES // STEP
DEPTH = 512
BLOCKS = WIN // LANES
SIDE = 4


def rotation(dy, dx):
    return [
        (y * SIDE + x, (y + dy) % SIDE * SIDE + (x + dx) % SIDE)
        for y in range(SIDE)
        for x in range(SIDE)
    ]


def prepare(
    groups, entries, station_ref, shift_ref, data_ref, out_ref, ask_ref, slot_ref, scratch, count
):
    list_size = station_ref.shape[1]
    owned = data_ref.shape[1]
    scratch[...] = jnp.zeros_like(scratch)
    for c in range(CH):
        x = data_ref[c].astype(jnp.float32)
        for q in range(TILES):
            width = min(LANES, DLEN - q * LANES)
            scratch[pl.ds(c * TILES + q, owned, stride=ROWS), 0:width] = x[
                :, q * LANES : q * LANES + width
            ]
    packed = scratch[...].astype(jnp.bfloat16)
    for d in range(out_ref.shape[0]):
        out_ref[d] = packed
    for g in range(groups):
        count[g] = 0
        for s in range(CAP):
            ask_ref[0, g * CAP + s] = 0
    for e in range(entries):
        station = station_ref[e // list_size, e % list_size]
        g = station // 32
        position = jnp.minimum(count[g], CAP - 1)
        count[g] = position + 1
        ask_ref[0, g * CAP + position] = station - g * 32
        slot_ref[0, e] = g * CAP + position
        slot_ref[1, e] = shift_ref[e // list_size, e % list_size]


def build_bands(shift_ref, templates_ref, band_ref, scale_ref, ones_ref, scratch):
    scratch[...] = jnp.zeros_like(scratch)
    list_size = templates_ref.shape[0]
    owned = templates_ref.shape[2]

    def step(k, carry):
        for c in range(CH):
            x = templates_ref[k, c].astype(jnp.float32)
            scratch[0:owned, 0:TLEN] = x
            energy = jnp.sum(x * x, axis=1, keepdims=True)
            scale = lax.rsqrt(energy / TLEN + EPS) / TLEN
            scale_ref[k, c] = jnp.broadcast_to(scale, (owned, LANES))
            for t in range(owned):
                moved = pltpu.roll(scratch[...], shift_ref[t, k] % STEP, 1)
                rows = jnp.broadcast_to(moved[t : t + 1, :], (STEP, DEPTH))
                band = pltpu.roll(rows, 0, 1, stride=1, stride_axis=0)
                place = pl.multiple_of((t * list_size + k) * STEP, STEP)
                band_ref[c, pl.ds(place, STEP), :] = band.astype(jnp.bfloat16)
        return carry

    lax.fori_loop(0, list_size, step, 0)
    r = lax.broadcasted_iota(jnp.int32, (LANES, LANES), 0)
    i = lax.broadcasted_iota(jnp.int32, (LANES, LANES), 1)
    kinds = (r >= i, r >= 0, r - i < TLEN - 384, r - i < TLEN - 512)
    for n, kind in enumerate(kinds):
        block = jnp.where(kind, 1.0, 0.0).astype(jnp.bfloat16)
        ones_ref[0:LANES, n * LANES : (n + 1) * LANES] = block
        ones_ref[LANES : 2 * LANES, n * LANES : (n + 1) * LANES] = block


def pick(*refs):
    asks, (data_ref, out_ref, sem) = refs[:SIDE], refs[SIDE:]
    me = lax.axis_index("st")
    y, x = me // SIDE, me % SIDE
    for dy in range(SIDE):
        for dx in range(SIDE):
            i = ((y + SIDE - dy) % SIDE) * SIDE + (x + SIDE - dx) % SIDE
            for s in range(CAP):
                station = asks[dy][dx, me * CAP + s]
                t = station // 2
                k = station - t * 2
                pltpu.make_async_copy(
                    data_ref.at[t, pl.ds(pl.multiple_of(k * ROWS, 8), ROWS)],
                    out_ref.at[i, pl.ds(s * ROWS, ROWS)],
                    sem,
                ).start()
    pltpu.make_async_copy(out_ref, out_ref, sem).wait()


def correlate(
    entries, slot_ref, data_ref, band_ref, scale_ref, ones_ref, out_ref,
    wide, turned, versions, squares, sums,
):
    list_size = entries // out_ref.shape[0]
    lane = lax.broadcasted_iota(jnp.int32, (ROWS, LANES), 1)
    lane8 = lax.broadcasted_iota(jnp.int32, (8, LANES), 1)
    totals = [jnp.zeros((8, LANES), jnp.float32) for _ in range(out_ref.shape[0])]
    for batch in range(entries // 8):
        for e in range(batch * 8, batch * 8 + 8):
            shift = slot_ref[1, e]
            slot = slot_ref[0, e]
            group = slot // CAP
            row = pl.multiple_of((slot - group * CAP) * ROWS, 8)
            record = data_ref[group, pl.ds(row, ROWS), :].astype(jnp.float32)
            base = e * PITCH
            wide[base : base + ROWS, :] = record
            wide[base + ROWS : base + PITCH, :] = jnp.zeros((PITCH - ROWS, LANES), jnp.float32)
            whole = shift // LANES
            part = shift - whole * LANES
            back = jnp.where(part == 0, 0, LANES - part)
            first = pltpu.roll(wide[pl.ds(base + whole, ROWS), :], back, 1)
            second = pltpu.roll(wide[pl.ds(base + whole + 1, ROWS), :], back, 1)
            y = jnp.where(lane < LANES - part, first, second)
            sq = y * y
            high = sq.astype(jnp.bfloat16)
            squares[e * ROWS : (e + 1) * ROWS, 0:LANES] = high
            squares[e * ROWS : (e + 1) * ROWS, LANES:] = (sq - high.astype(jnp.float32)).astype(
                jnp.bfloat16
            )
            start = e * PITCH
            versions[0, start : start + ROWS, :] = record
            for k in range(1, PHASES):
                moved = pltpu.roll(record, LANES - k * STEP, 1)
                turned[k - 1, start : start + ROWS, :] = moved
                versions[k, start : start + ROWS, :] = jnp.where(
                    lane < LANES - k * STEP, moved, turned[k - 1, start + 1 : start + 1 + ROWS, :]
                )
        part = slice(batch * 8 * ROWS, (batch + 1) * 8 * ROWS)
        sums[part, :] = jnp.dot(
            squares[part, :], ones_ref[...], preferred_element_type=jnp.float32
        )
        for c in range(CH):
            frames = []
            for n in range(8):
                e = batch * 8 + n
                coarse = slot_ref[1, e] // STEP
                for h in range(PHASES):
                    at = coarse + h
                    version = at % PHASES
                    start = e * PITCH + c * TILES + at // PHASES
                    frames.append(
                        jnp.concatenate(
                            [
                                versions[version, pl.ds(start + q, 8), :]
                                for q in range(DEPTH // LANES)
                            ],
                            axis=1,
                        )
                    )
            left = jnp.concatenate(frames, axis=0).astype(jnp.bfloat16)
            product = lax.dot_general(
                left,
                band_ref[c, batch * 8 * STEP : (batch + 1) * 8 * STEP, :],
                (((1,), (1,)), ((), ())),
                preferred_element_type=jnp.float32,
            )
            for n in range(8):
                e = batch * 8 + n
                column = (n // PHASES) * LANES
                raw = None
                for h in range(PHASES):
                    piece = product[
                        (n * PHASES + h) * 8 : (n * PHASES + h + 1) * 8, column : column + LANES
                    ]
                    turn = (h - n) % PHASES * STEP
                    if turn:
                        piece = pltpu.roll(piece, turn, 1)
                    raw = piece if raw is None else jnp.where(lane8 < h * STEP, raw, piece)
                start = e * ROWS + c * TILES
                energy = (
                    sums[start : start + 8, 0:LANES]
                    + sums[start + 1 : start + 9, LANES : 2 * LANES]
                    + sums[start + 2 : start + 10, LANES : 2 * LANES]
                    + sums[start + 3 : start + 11, 2 * LANES : 3 * LANES]
                    + sums[start + 4 : start + 12, 3 * LANES :]
                )
                level = lax.rsqrt(energy / TLEN + EPS)
                totals[e // list_size] = totals[e // list_size] + raw * level * scale_ref[
                    e % list_size, c, e // list_size : e // list_size + 1, :
                ]
    for t, total in enumerate(totals):
        for b in range(BLOCKS):
            out_ref[t : t + 1, b * LANES : (b + 1) * LANES] = total[b : b + 1, :]


def shards(continuous, templates, station_list, moveouts):
    groups = lax.axis_size("st")
    peers = lax.axis_size("tp")
    owned = continuous.shape[0]
    template_count, list_size = station_list.shape
    entries = template_count * list_size
    smem = pl.BlockSpec(memory_space=pltpu.SMEM)
    vmem = pl.BlockSpec(memory_space=pltpu.VMEM)
    anywhere = pl.BlockSpec(memory_space=pl.ANY)

    def from_hbm(array):
        return pltpu.with_memory_space_constraint(array, pltpu.HBM)

    def params(mebibytes):
        return pltpu.CompilerParams(vmem_limit_bytes=mebibytes * 2**20)

    spread, asked, slots = pl.pallas_call(
        lambda *refs: prepare(groups, entries, *refs),
        out_shape=(
            jax.ShapeDtypeStruct((peers, owned * ROWS, LANES), jnp.bfloat16),
            jax.ShapeDtypeStruct((1, LANES), jnp.int32),
            pltpu.SMEM((2, LANES), jnp.int32),
        ),
        in_specs=[smem, smem, vmem],
        out_specs=(vmem, smem, smem),
        scratch_shapes=[
            pltpu.VMEM((owned * ROWS, LANES), jnp.float32),
            pltpu.SMEM((groups,), jnp.int32),
        ],
        compiler_params=params(4),
        name="prepare",
    )(from_hbm(station_list), from_hbm(moveouts), from_hbm(jnp.swapaxes(continuous, 0, 1)))
    along_x = [asked] + [lax.ppermute(asked, "st", rotation(0, d)) for d in range(1, SIDE)]
    row = jnp.concatenate(along_x, axis=0)
    asks = [row] + [lax.ppermute(row, "st", rotation(d, 0)) for d in range(1, SIDE)]
    group_rows = lax.all_to_all(spread, "tp", split_axis=0, concat_axis=0, tiled=True)
    bands, scales, ones = pl.pallas_call(
        build_bands,
        out_shape=(
            jax.ShapeDtypeStruct((CH, entries * STEP, DEPTH), jnp.bfloat16),
            jax.ShapeDtypeStruct((list_size, CH, template_count, LANES), jnp.float32),
            jax.ShapeDtypeStruct((2 * LANES, 4 * LANES), jnp.bfloat16),
        ),
        in_specs=[smem, vmem],
        out_specs=(vmem, vmem, vmem),
        scratch_shapes=[pltpu.VMEM((8, DEPTH), jnp.float32)],
        compiler_params=params(12),
        name="bands",
    )(from_hbm(moveouts), from_hbm(jnp.transpose(templates, (1, 2, 0, 3))))
    picked = pl.pallas_call(
        pick,
        out_shape=jax.ShapeDtypeStruct((groups, CAP * ROWS, LANES), jnp.bfloat16),
        in_specs=[smem] * SIDE + [anywhere],
        out_specs=anywhere,
        scratch_shapes=[pltpu.SemaphoreType.DMA],
        compiler_params=params(2),
        name="pick",
    )(*asks, group_rows)
    records = lax.all_to_all(picked, "st", split_axis=0, concat_axis=0, tiled=True)
    return pl.pallas_call(
        lambda *refs: correlate(entries, *refs),
        out_shape=jax.ShapeDtypeStruct((template_count, WIN), jnp.float32),
        in_specs=[smem, vmem, vmem, vmem, vmem],
        out_specs=vmem,
        scratch_shapes=[
            pltpu.VMEM((entries * PITCH, LANES), jnp.float32),
            pltpu.VMEM((PHASES - 1, entries * PITCH, LANES), jnp.float32),
            pltpu.VMEM((PHASES, entries * PITCH, LANES), jnp.float32),
            pltpu.VMEM((entries * ROWS, 2 * LANES), jnp.bfloat16),
            pltpu.VMEM((entries * ROWS, 4 * LANES), jnp.float32),
        ],
        compiler_params=params(20),
        name="correlate",
    )(slots, records, bands, scales, ones)


def solution(mesh):
    placed = (
        P(("st", "tp"), None, None),
        P(("st", "tp"), None, None, None),
        P(("st", "tp"), None),
        P(("st", "tp"), None),
    )
    return jax.shard_map(
        shards, mesh=mesh, in_specs=placed, out_specs=P(("st", "tp"), None), check_vma=False
    )
```

```python
import jax
import jax.numpy as jnp
from jax import lax
from jax.experimental import pallas as pl
from jax.experimental.pallas import tpu as pltpu
from jax.sharding import PartitionSpec as P

WIN = 768
TLEN = 400
CH = 3
DLEN = 1424
EPS = 1e-05
LANES = 128
TILES = 12
ROWS = 40
CAP = 3
PITCH = 48
STEP = 32
PHASES = LANES // STEP
DEPTH = 512
BLOCKS = WIN // LANES
SIDE = 4


def rotation(dy, dx):
    return [
        (y * SIDE + x, (y + dy) % SIDE * SIDE + (x + dx) % SIDE)
        for y in range(SIDE)
        for x in range(SIDE)
    ]


def prepare(
    groups, entries, station_ref, shift_ref, data_ref, out_ref, ask_ref, slot_ref, scratch, count
):
    list_size = station_ref.shape[1]
    owned = data_ref.shape[1]
    scratch[...] = jnp.zeros_like(scratch)
    for c in range(CH):
        x = data_ref[c].astype(jnp.float32)
        for q in range(TILES):
            width = min(LANES, DLEN - q * LANES)
            scratch[pl.ds(c * TILES + q, owned, stride=ROWS), 0:width] = x[
                :, q * LANES : q * LANES + width
            ]
    packed = scratch[...].astype(jnp.bfloat16)
    for d in range(out_ref.shape[0]):
        out_ref[d] = packed
    for g in range(groups):
        count[g] = 0
        for s in range(CAP):
            ask_ref[0, g * CAP + s] = 0
    for e in range(entries):
        station = station_ref[e // list_size, e % list_size]
        g = station // 32
        position = jnp.minimum(count[g], CAP - 1)
        count[g] = position + 1
        ask_ref[0, g * CAP + position] = station - g * 32
        slot_ref[0, e] = g * CAP + position
        slot_ref[1, e] = shift_ref[e // list_size, e % list_size]


def build_bands(shift_ref, templates_ref, band_ref, scale_ref, ones_ref, scratch):
    scratch[...] = jnp.zeros_like(scratch)
    list_size = templates_ref.shape[0]
    owned = templates_ref.shape[2]

    def step(k, carry):
        for c in range(CH):
            x = templates_ref[k, c].astype(jnp.float32)
            scratch[0:owned, 0:TLEN] = x
            energy = jnp.sum(x * x, axis=1, keepdims=True)
            scale = lax.rsqrt(energy / TLEN + EPS) / TLEN
            scale_ref[k, c] = jnp.broadcast_to(scale, (owned, LANES))
            for t in range(owned):
                moved = pltpu.roll(scratch[...], shift_ref[t, k] % STEP, 1)
                rows = jnp.broadcast_to(moved[t : t + 1, :], (STEP, DEPTH))
                band = pltpu.roll(rows, 0, 1, stride=1, stride_axis=0)
                place = pl.multiple_of((t * list_size + k) * STEP, STEP)
                band_ref[c, pl.ds(place, STEP), :] = band.astype(jnp.bfloat16)
        return carry

    lax.fori_loop(0, list_size, step, 0)
    r = lax.broadcasted_iota(jnp.int32, (LANES, LANES), 0)
    i = lax.broadcasted_iota(jnp.int32, (LANES, LANES), 1)
    kinds = (r >= i, r >= 0, r - i < TLEN - 384, r - i < TLEN - 512)
    for n, kind in enumerate(kinds):
        block = jnp.where(kind, 1.0, 0.0).astype(jnp.bfloat16)
        ones_ref[0:LANES, n * LANES : (n + 1) * LANES] = block
        ones_ref[LANES : 2 * LANES, n * LANES : (n + 1) * LANES] = block


def pick(ask_ref, data_ref, out_ref, held, sem):
    me = lax.axis_index("st")
    y, x = me // SIDE, me % SIDE
    for dy in range(SIDE):
        for dx in range(SIDE):
            n = dy * SIDE + dx
            i = ((y + SIDE - dy) % SIDE) * SIDE + (x + SIDE - dx) % SIDE
            for s in range(CAP):
                station = ask_ref[n, me * CAP + s]
                t = station // 2
                row = pl.multiple_of((station - t * 2) * ROWS, 8)
                held[n, s * ROWS : (s + 1) * ROWS, :] = data_ref[t, pl.ds(row, ROWS), :]
            pltpu.make_async_copy(held.at[n], out_ref.at[i], sem).start()
    pltpu.make_async_copy(out_ref, out_ref, sem).wait()


def correlate(
    entries, slot_ref, data_ref, band_ref, scale_ref, ones_ref, out_ref,
    wide, turned, versions, squares, sums,
):
    list_size = entries // out_ref.shape[0]
    lane = lax.broadcasted_iota(jnp.int32, (ROWS, LANES), 1)
    lane8 = lax.broadcasted_iota(jnp.int32, (8, LANES), 1)
    totals = [jnp.zeros((8, LANES), jnp.float32) for _ in range(out_ref.shape[0])]
    for batch in range(entries // 8):
        for e in range(batch * 8, batch * 8 + 8):
            shift = slot_ref[1, e]
            slot = slot_ref[0, e]
            group = slot // CAP
            row = pl.multiple_of((slot - group * CAP) * ROWS, 8)
            record = data_ref[group, pl.ds(row, ROWS), :].astype(jnp.float32)
            base = e * PITCH
            wide[base : base + ROWS, :] = record
            wide[base + ROWS : base + PITCH, :] = jnp.zeros((PITCH - ROWS, LANES), jnp.float32)
            whole = shift // LANES
            part = shift - whole * LANES
            back = jnp.where(part == 0, 0, LANES - part)
            first = pltpu.roll(wide[pl.ds(base + whole, ROWS), :], back, 1)
            second = pltpu.roll(wide[pl.ds(base + whole + 1, ROWS), :], back, 1)
            y = jnp.where(lane < LANES - part, first, second)
            sq = y * y
            high = sq.astype(jnp.bfloat16)
            squares[e * ROWS : (e + 1) * ROWS, 0:LANES] = high
            squares[e * ROWS : (e + 1) * ROWS, LANES:] = (sq - high.astype(jnp.float32)).astype(
                jnp.bfloat16
            )
            start = e * PITCH
            versions[0, start : start + ROWS, :] = record
            for k in range(1, PHASES):
                moved = pltpu.roll(record, LANES - k * STEP, 1)
                turned[k - 1, start : start + ROWS, :] = moved
                versions[k, start : start + ROWS, :] = jnp.where(
                    lane < LANES - k * STEP, moved, turned[k - 1, start + 1 : start + 1 + ROWS, :]
                )
        part = slice(batch * 8 * ROWS, (batch + 1) * 8 * ROWS)
        sums[part, :] = jnp.dot(
            squares[part, :], ones_ref[...], preferred_element_type=jnp.float32
        )
        for c in range(CH):
            frames = []
            for n in range(8):
                e = batch * 8 + n
                coarse = slot_ref[1, e] // STEP
                for h in range(PHASES):
                    at = coarse + h
                    version = at % PHASES
                    start = e * PITCH + c * TILES + at // PHASES
                    frames.append(
                        jnp.concatenate(
                            [
                                versions[version, pl.ds(start + q, 8), :]
                                for q in range(DEPTH // LANES)
                            ],
                            axis=1,
                        )
                    )
            left = jnp.concatenate(frames, axis=0).astype(jnp.bfloat16)
            product = lax.dot_general(
                left,
                band_ref[c, batch * 8 * STEP : (batch + 1) * 8 * STEP, :],
                (((1,), (1,)), ((), ())),
                preferred_element_type=jnp.float32,
            )
            for n in range(8):
                e = batch * 8 + n
                column = (n // PHASES) * LANES
                raw = None
                for h in range(PHASES):
                    piece = product[
                        (n * PHASES + h) * 8 : (n * PHASES + h + 1) * 8, column : column + LANES
                    ]
                    turn = (h - n) % PHASES * STEP
                    if turn:
                        piece = pltpu.roll(piece, turn, 1)
                    raw = piece if raw is None else jnp.where(lane8 < h * STEP, raw, piece)
                start = e * ROWS + c * TILES
                energy = (
                    sums[start : start + 8, 0:LANES]
                    + sums[start + 1 : start + 9, LANES : 2 * LANES]
                    + sums[start + 2 : start + 10, LANES : 2 * LANES]
                    + sums[start + 3 : start + 11, 2 * LANES : 3 * LANES]
                    + sums[start + 4 : start + 12, 3 * LANES :]
                )
                level = lax.rsqrt(energy / TLEN + EPS)
                totals[e // list_size] = totals[e // list_size] + raw * level * scale_ref[
                    e % list_size, c, e // list_size : e // list_size + 1, :
                ]
    for t, total in enumerate(totals):
        for b in range(BLOCKS):
            out_ref[t : t + 1, b * LANES : (b + 1) * LANES] = total[b : b + 1, :]


def shards(continuous, templates, station_list, moveouts):
    groups = lax.axis_size("st")
    peers = lax.axis_size("tp")
    owned = continuous.shape[0]
    template_count, list_size = station_list.shape
    entries = template_count * list_size
    smem = pl.BlockSpec(memory_space=pltpu.SMEM)
    vmem = pl.BlockSpec(memory_space=pltpu.VMEM)
    anywhere = pl.BlockSpec(memory_space=pl.ANY)

    def from_hbm(array):
        return pltpu.with_memory_space_constraint(array, pltpu.HBM)

    def params(mebibytes):
        return pltpu.CompilerParams(vmem_limit_bytes=mebibytes * 2**20)

    spread, asked, slots = pl.pallas_call(
        lambda *refs: prepare(groups, entries, *refs),
        out_shape=(
            jax.ShapeDtypeStruct((peers, owned * ROWS, LANES), jnp.bfloat16),
            jax.ShapeDtypeStruct((1, LANES), jnp.int32),
            pltpu.SMEM((2, LANES), jnp.int32),
        ),
        in_specs=[smem, smem, vmem],
        out_specs=(vmem, smem, smem),
        scratch_shapes=[
            pltpu.VMEM((owned * ROWS, LANES), jnp.float32),
            pltpu.SMEM((groups,), jnp.int32),
        ],
        compiler_params=params(4),
        name="prepare",
    )(from_hbm(station_list), from_hbm(moveouts), from_hbm(jnp.swapaxes(continuous, 0, 1)))
    along_x = [asked] + [lax.ppermute(asked, "st", rotation(0, d)) for d in range(1, SIDE)]
    row = jnp.concatenate(along_x, axis=0)
    asks = [row] + [lax.ppermute(row, "st", rotation(d, 0)) for d in range(1, SIDE)]
    group_rows = lax.all_to_all(spread, "tp", split_axis=0, concat_axis=0, tiled=True)
    bands, scales, ones = pl.pallas_call(
        build_bands,
        out_shape=(
            jax.ShapeDtypeStruct((CH, entries * STEP, DEPTH), jnp.bfloat16),
            jax.ShapeDtypeStruct((list_size, CH, template_count, LANES), jnp.float32),
            jax.ShapeDtypeStruct((2 * LANES, 4 * LANES), jnp.bfloat16),
        ),
        in_specs=[smem, vmem],
        out_specs=(vmem, vmem, vmem),
        scratch_shapes=[pltpu.VMEM((8, DEPTH), jnp.float32)],
        compiler_params=params(12),
        name="bands",
    )(from_hbm(moveouts), from_hbm(jnp.transpose(templates, (1, 2, 0, 3))))
    picked = pl.pallas_call(
        pick,
        out_shape=jax.ShapeDtypeStruct((groups, CAP * ROWS, LANES), jnp.bfloat16),
        in_specs=[smem, vmem],
        out_specs=anywhere,
        scratch_shapes=[
            pltpu.VMEM((groups, CAP * ROWS, LANES), jnp.bfloat16),
            pltpu.SemaphoreType.DMA,
        ],
        compiler_params=params(2),
        name="pick",
    )(jnp.concatenate(asks, axis=0), group_rows)
    records = lax.all_to_all(picked, "st", split_axis=0, concat_axis=0, tiled=True)
    return pl.pallas_call(
        lambda *refs: correlate(entries, *refs),
        out_shape=jax.ShapeDtypeStruct((template_count, WIN), jnp.float32),
        in_specs=[smem, vmem, vmem, vmem, vmem],
        out_specs=vmem,
        scratch_shapes=[
            pltpu.VMEM((entries * PITCH, LANES), jnp.float32),
            pltpu.VMEM((PHASES - 1, entries * PITCH, LANES), jnp.float32),
            pltpu.VMEM((PHASES, entries * PITCH, LANES), jnp.float32),
            pltpu.VMEM((entries * ROWS, 2 * LANES), jnp.bfloat16),
            pltpu.VMEM((entries * ROWS, 4 * LANES), jnp.float32),
        ],
        compiler_params=params(20),
        name="correlate",
    )(slots, records, bands, scales, ones)


def solution(mesh):
    placed = (
        P(("st", "tp"), None, None),
        P(("st", "tp"), None, None, None),
        P(("st", "tp"), None),
        P(("st", "tp"), None),
    )
    return jax.shard_map(
        shards, mesh=mesh, in_specs=placed, out_specs=P(("st", "tp"), None), check_vma=False
    )
```

```python
import jax
import jax.numpy as jnp
from jax import lax
from jax.experimental import pallas as pl
from jax.experimental.pallas import tpu as pltpu
from jax.sharding import PartitionSpec as P

WIN = 768
TLEN = 400
CH = 3
DLEN = 1424
EPS = 1e-05
LANES = 128
TILES = 12
ROWS = 40
CAP = 3
PITCH = 48
STEP = 32
PHASES = LANES // STEP
DEPTH = 512
BLOCKS = WIN // LANES
SIDE = 4


def partners(dy, dx):
    return [
        (y * SIDE + x, (y ^ dy) * SIDE + (x ^ dx))
        for y in range(SIDE)
        for x in range(SIDE)
    ]


def prepare(
    groups, entries, station_ref, shift_ref, data_ref, out_ref, ask_ref, slot_ref, scratch, count
):
    list_size = station_ref.shape[1]
    owned = data_ref.shape[1]
    scratch[...] = jnp.zeros_like(scratch)
    for c in range(CH):
        x = data_ref[c].astype(jnp.float32)
        for q in range(TILES):
            width = min(LANES, DLEN - q * LANES)
            scratch[pl.ds(c * TILES + q, owned, stride=ROWS), 0:width] = x[
                :, q * LANES : q * LANES + width
            ]
    packed = scratch[...].astype(jnp.bfloat16)
    for d in range(out_ref.shape[0]):
        out_ref[d] = packed
    for g in range(groups):
        count[g] = 0
        for s in range(CAP):
            ask_ref[0, g * CAP + s] = 0
    for e in range(entries):
        station = station_ref[e // list_size, e % list_size]
        g = station // 32
        position = jnp.minimum(count[g], CAP - 1)
        count[g] = position + 1
        ask_ref[0, g * CAP + position] = station - g * 32
        slot_ref[0, e] = g * CAP + position
        slot_ref[1, e] = shift_ref[e // list_size, e % list_size]


def build_bands(shift_ref, templates_ref, band_ref, scale_ref, ones_ref, scratch):
    scratch[...] = jnp.zeros_like(scratch)
    list_size = templates_ref.shape[0]
    owned = templates_ref.shape[2]

    def step(k, carry):
        for c in range(CH):
            x = templates_ref[k, c].astype(jnp.float32)
            scratch[0:owned, 0:TLEN] = x
            energy = jnp.sum(x * x, axis=1, keepdims=True)
            scale = lax.rsqrt(energy / TLEN + EPS) / TLEN
            scale_ref[k, c] = jnp.broadcast_to(scale, (owned, LANES))
            for t in range(owned):
                moved = pltpu.roll(scratch[...], shift_ref[t, k] % STEP, 1)
                rows = jnp.broadcast_to(moved[t : t + 1, :], (STEP, DEPTH))
                band = pltpu.roll(rows, 0, 1, stride=1, stride_axis=0)
                place = pl.multiple_of((t * list_size + k) * STEP, STEP)
                band_ref[c, pl.ds(place, STEP), :] = band.astype(jnp.bfloat16)
        return carry

    lax.fori_loop(0, list_size, step, 0)
    r = lax.broadcasted_iota(jnp.int32, (LANES, LANES), 0)
    i = lax.broadcasted_iota(jnp.int32, (LANES, LANES), 1)
    kinds = (r >= i, r >= 0, r - i < TLEN - 384, r - i < TLEN - 512)
    for n, kind in enumerate(kinds):
        block = jnp.where(kind, 1.0, 0.0).astype(jnp.bfloat16)
        ones_ref[0:LANES, n * LANES : (n + 1) * LANES] = block
        ones_ref[LANES : 2 * LANES, n * LANES : (n + 1) * LANES] = block


def pick(ask_ref, data_ref, out_ref, held, sem):
    me = lax.axis_index("st")
    y, x = me // SIDE, me % SIDE
    for dy in range(SIDE):
        for dx in range(SIDE):
            n = dy * SIDE + dx
            i = (y ^ dy) * SIDE + (x ^ dx)
            for s in range(CAP):
                station = ask_ref[n, me * CAP + s]
                t = station // 2
                row = pl.multiple_of((station - t * 2) * ROWS, 8)
                held[n, s * ROWS : (s + 1) * ROWS, :] = data_ref[t, pl.ds(row, ROWS), :]
            pltpu.make_async_copy(held.at[n], out_ref.at[i], sem).start()
    pltpu.make_async_copy(out_ref, out_ref, sem).wait()


def correlate(
    entries, slot_ref, data_ref, band_ref, scale_ref, ones_ref, out_ref,
    wide, turned, versions, squares, sums,
):
    list_size = entries // out_ref.shape[0]
    lane = lax.broadcasted_iota(jnp.int32, (ROWS, LANES), 1)
    lane8 = lax.broadcasted_iota(jnp.int32, (8, LANES), 1)
    totals = [jnp.zeros((8, LANES), jnp.float32) for _ in range(out_ref.shape[0])]
    for batch in range(entries // 8):
        for e in range(batch * 8, batch * 8 + 8):
            shift = slot_ref[1, e]
            slot = slot_ref[0, e]
            group = slot // CAP
            row = pl.multiple_of((slot - group * CAP) * ROWS, 8)
            record = data_ref[group, pl.ds(row, ROWS), :].astype(jnp.float32)
            base = e * PITCH
            wide[base : base + ROWS, :] = record
            wide[base + ROWS : base + PITCH, :] = jnp.zeros((PITCH - ROWS, LANES), jnp.float32)
            whole = shift // LANES
            part = shift - whole * LANES
            back = jnp.where(part == 0, 0, LANES - part)
            first = pltpu.roll(wide[pl.ds(base + whole, ROWS), :], back, 1)
            second = pltpu.roll(wide[pl.ds(base + whole + 1, ROWS), :], back, 1)
            y = jnp.where(lane < LANES - part, first, second)
            sq = y * y
            high = sq.astype(jnp.bfloat16)
            squares[e * ROWS : (e + 1) * ROWS, 0:LANES] = high
            squares[e * ROWS : (e + 1) * ROWS, LANES:] = (sq - high.astype(jnp.float32)).astype(
                jnp.bfloat16
            )
            start = e * PITCH
            versions[0, start : start + ROWS, :] = record
            for k in range(1, PHASES):
                moved = pltpu.roll(record, LANES - k * STEP, 1)
                turned[k - 1, start : start + ROWS, :] = moved
                versions[k, start : start + ROWS, :] = jnp.where(
                    lane < LANES - k * STEP, moved, turned[k - 1, start + 1 : start + 1 + ROWS, :]
                )
        part = slice(batch * 8 * ROWS, (batch + 1) * 8 * ROWS)
        sums[part, :] = jnp.dot(
            squares[part, :], ones_ref[...], preferred_element_type=jnp.float32
        )
        for c in range(CH):
            frames = []
            for n in range(8):
                e = batch * 8 + n
                coarse = slot_ref[1, e] // STEP
                for h in range(PHASES):
                    at = coarse + h
                    version = at % PHASES
                    start = e * PITCH + c * TILES + at // PHASES
                    frames.append(
                        jnp.concatenate(
                            [
                                versions[version, pl.ds(start + q, 8), :]
                                for q in range(DEPTH // LANES)
                            ],
                            axis=1,
                        )
                    )
            left = jnp.concatenate(frames, axis=0).astype(jnp.bfloat16)
            product = lax.dot_general(
                left,
                band_ref[c, batch * 8 * STEP : (batch + 1) * 8 * STEP, :],
                (((1,), (1,)), ((), ())),
                preferred_element_type=jnp.float32,
            )
            for n in range(8):
                e = batch * 8 + n
                column = (n // PHASES) * LANES
                raw = None
                for h in range(PHASES):
                    piece = product[
                        (n * PHASES + h) * 8 : (n * PHASES + h + 1) * 8, column : column + LANES
                    ]
                    turn = (h - n) % PHASES * STEP
                    if turn:
                        piece = pltpu.roll(piece, turn, 1)
                    raw = piece if raw is None else jnp.where(lane8 < h * STEP, raw, piece)
                start = e * ROWS + c * TILES
                energy = (
                    sums[start : start + 8, 0:LANES]
                    + sums[start + 1 : start + 9, LANES : 2 * LANES]
                    + sums[start + 2 : start + 10, LANES : 2 * LANES]
                    + sums[start + 3 : start + 11, 2 * LANES : 3 * LANES]
                    + sums[start + 4 : start + 12, 3 * LANES :]
                )
                level = lax.rsqrt(energy / TLEN + EPS)
                totals[e // list_size] = totals[e // list_size] + raw * level * scale_ref[
                    e % list_size, c, e // list_size : e // list_size + 1, :
                ]
    for t, total in enumerate(totals):
        for b in range(BLOCKS):
            out_ref[t : t + 1, b * LANES : (b + 1) * LANES] = total[b : b + 1, :]


def shards(continuous, templates, station_list, moveouts):
    groups = lax.axis_size("st")
    peers = lax.axis_size("tp")
    owned = continuous.shape[0]
    template_count, list_size = station_list.shape
    entries = template_count * list_size
    smem = pl.BlockSpec(memory_space=pltpu.SMEM)
    vmem = pl.BlockSpec(memory_space=pltpu.VMEM)
    anywhere = pl.BlockSpec(memory_space=pl.ANY)

    def from_hbm(array):
        return pltpu.with_memory_space_constraint(array, pltpu.HBM)

    def params(mebibytes):
        return pltpu.CompilerParams(vmem_limit_bytes=mebibytes * 2**20)

    spread, asked, slots = pl.pallas_call(
        lambda *refs: prepare(groups, entries, *refs),
        out_shape=(
            jax.ShapeDtypeStruct((peers, owned * ROWS, LANES), jnp.bfloat16),
            jax.ShapeDtypeStruct((1, LANES), jnp.int32),
            pltpu.SMEM((2, LANES), jnp.int32),
        ),
        in_specs=[smem, smem, vmem],
        out_specs=(vmem, smem, smem),
        scratch_shapes=[
            pltpu.VMEM((owned * ROWS, LANES), jnp.float32),
            pltpu.SMEM((groups,), jnp.int32),
        ],
        compiler_params=params(4),
        name="prepare",
    )(from_hbm(station_list), from_hbm(moveouts), from_hbm(jnp.swapaxes(continuous, 0, 1)))
    along_x = [asked] + [lax.ppermute(asked, "st", partners(0, d)) for d in range(1, SIDE)]
    row = jnp.concatenate(along_x, axis=0)
    asks = [row] + [lax.ppermute(row, "st", partners(d, 0)) for d in range(1, SIDE)]
    group_rows = lax.all_to_all(spread, "tp", split_axis=0, concat_axis=0, tiled=True)
    bands, scales, ones = pl.pallas_call(
        build_bands,
        out_shape=(
            jax.ShapeDtypeStruct((CH, entries * STEP, DEPTH), jnp.bfloat16),
            jax.ShapeDtypeStruct((list_size, CH, template_count, LANES), jnp.float32),
            jax.ShapeDtypeStruct((2 * LANES, 4 * LANES), jnp.bfloat16),
        ),
        in_specs=[smem, vmem],
        out_specs=(vmem, vmem, vmem),
        scratch_shapes=[pltpu.VMEM((8, DEPTH), jnp.float32)],
        compiler_params=params(12),
        name="bands",
    )(from_hbm(moveouts), from_hbm(jnp.transpose(templates, (1, 2, 0, 3))))
    picked = pl.pallas_call(
        pick,
        out_shape=jax.ShapeDtypeStruct((groups, CAP * ROWS, LANES), jnp.bfloat16),
        in_specs=[smem, vmem],
        out_specs=anywhere,
        scratch_shapes=[
            pltpu.VMEM((groups, CAP * ROWS, LANES), jnp.bfloat16),
            pltpu.SemaphoreType.DMA,
        ],
        compiler_params=params(2),
        name="pick",
    )(jnp.concatenate(asks, axis=0), group_rows)
    records = lax.all_to_all(picked, "st", split_axis=0, concat_axis=0, tiled=True)
    return pl.pallas_call(
        lambda *refs: correlate(entries, *refs),
        out_shape=jax.ShapeDtypeStruct((template_count, WIN), jnp.float32),
        in_specs=[smem, vmem, vmem, vmem, vmem],
        out_specs=vmem,
        scratch_shapes=[
            pltpu.VMEM((entries * PITCH, LANES), jnp.float32),
            pltpu.VMEM((PHASES - 1, entries * PITCH, LANES), jnp.float32),
            pltpu.VMEM((PHASES, entries * PITCH, LANES), jnp.float32),
            pltpu.VMEM((entries * ROWS, 2 * LANES), jnp.bfloat16),
            pltpu.VMEM((entries * ROWS, 4 * LANES), jnp.float32),
        ],
        compiler_params=params(20),
        name="correlate",
    )(slots, records, bands, scales, ones)


def solution(mesh):
    placed = (
        P(("st", "tp"), None, None),
        P(("st", "tp"), None, None, None),
        P(("st", "tp"), None),
        P(("st", "tp"), None),
    )
    return jax.shard_map(
        shards, mesh=mesh, in_specs=placed, out_specs=P(("st", "tp"), None), check_vma=False
    )
```
